32 devices in a mesh: dp: 4 (over z), context: 8 (over y, x, core).
Axes of the slice: x: 2, y: 2, z: 4, core: 2. Of those that a mesh axis runs over, the one named last changes fastest.
Arguments:
- inputs: bfloat16 [4, 1024, 4096], P('dp', 'context'), may hold values from -6 to 6
- cotangent: bfloat16 [4, 1024, 4096], P('dp', 'context'), may hold values from -6 to 6
- rate: float32 [16, 4096], replicated, may hold values from 0 to 1, as said below
- residues: float32 [16, 4096], replicated, may hold values from -3 to 3
Outputs:
- grad_inputs: bfloat16 [4, 1024, 4096], P('dp', 'context')
- grad_residues: float32 [16, 4096], P(None, 'dp')
- grad_rate: float32 [16, 4096], P(None, 'dp')
The draws below stay inside these ranges and needn't reach their ends.
Inputs may be any that keep to these rules, and one draw needn't show every extreme that they name: Every rate is positive.
All inputs are finite; a program needn't handle non-finite values.
Results may differ from the reference program's by a relative error of at most 0.001.
Values sent between devices are 32-bit elements; how exact they have to be, the bound alone decides.
No kernel may reach another device: no remote copies, remote signals or barrier semaphores. Data moves between devices by JAX's collectives and lax.ppermute only.
A program may use at most 192 MiB of HBM per device.

```python
import math
import jax
import jax.numpy as jnp
from jax import lax

D = 4096
ORDER = 16
BATCH = 4
LENGTH = 1024


def modal_draw(key):
    key_rate, key_res = jax.random.split(jax.random.fold_in(key, 4242))
    unit = jax.random.uniform(key_rate, (ORDER, D), jnp.float32)
    lowest = 0.2 / LENGTH
    highest = 1.0
    spread = jax.random.truncated_normal(key_res, -4.0, 4.0, (ORDER, D), jnp.float32)
    rate_vals = jnp.exp(jnp.log(lowest) + unit * (jnp.log(highest) - jnp.log(lowest)))
    res_vals = 0.5 * spread * jnp.sqrt(2.0 * rate_vals)
    return (rate_vals, res_vals)


def draw_rate(key, part):
    return modal_draw(key)[0]


def draw_residues(key, part):
    return modal_draw(key)[1]


def strengthened(drawn, stream_key, source, target, blocks, factor):
    def block_of(dim):
        return (jnp.arange(drawn.shape[dim]) // (drawn.shape[dim] // blocks)).reshape((-1,) + (1,) * (drawn.ndim - 1 - dim))

    first = jax.random.permutation(stream_key, blocks)[block_of(target)]
    second = (block_of(target) + blocks // 2) % blocks
    return jnp.where((block_of(source) == first) | (block_of(source) == second), factor * drawn, drawn)


def steps_of(rng, dims, shards, least, high):
    def one(axis_at, shards_of):
        draws = jax.random.uniform(jax.random.fold_in(jax.random.fold_in(rng, 6), axis_at), (shards_of,), jnp.float32, least / len(shards), high / len(shards))
        return jnp.repeat(jnp.exp(draws), dims[axis_at] // shards_of).reshape((-1,) + (1,) * (len(dims) - axis_at - 1))

    level = one(*shards[0])
    for cut in shards[1:]:
        level = level * one(*cut)
    return level


def normal_values(key, extent, scale, most, pieces=(), dtype=jnp.bfloat16):
    result = jax.random.normal(key, extent, jnp.float32) * scale
    if len(pieces) > 0:
        result = steps_of(key, extent, pieces, -0.22, 0.18) * result
    return jnp.clip(result, min=-most, max=most).astype(dtype)


def noise_with(stream_key, extent, scale, limit, cuts, heavy, dtype=jnp.bfloat16):
    drawn = scale * jax.random.normal(stream_key, extent, jnp.float32)
    if cuts:
        drawn = drawn * steps_of(stream_key, extent, cuts, -0.22, 0.18)
    return jnp.clip(strengthened(drawn, jax.random.fold_in(stream_key, 3), *heavy), -limit, limit).astype(dtype)


def setup_inputs(seed: int = 0) -> dict:
    arg_keys = jax.random.split(jax.random.key(seed), 5)
    inputs = noise_with(arg_keys[0], (BATCH, LENGTH, D), 1.0, 6.0, ((0, 4), (1, 8)), (0, 2, 4, 2.0))
    cotangent = normal_values(arg_keys[1], (BATCH, LENGTH, D), 1.0, 6.0, ((0, 4), (1, 8)))
    rate = draw_rate(jax.random.fold_in(arg_keys[4], 71), 0)
    residues = draw_residues(jax.random.fold_in(arg_keys[4], 71), 0)
    return dict(inputs=inputs, cotangent=cotangent, rate=rate, residues=residues)


def channel_block(inputs_blk, cotangent_blk, rate_blk, residues_blk):
    decay_step = jnp.exp(-rate_blk)
    input_vals = inputs_blk.astype(jnp.float32)
    cotan_vals = cotangent_blk.astype(jnp.float32)

    def forward_step(carry, row):
        new_state = decay_step * carry + row[None, :]
        return (new_state, carry)
    zero_state = jnp.zeros_like(decay_step)
    last_state, prev_states = lax.scan(forward_step, zero_state, input_vals)

    def backward_step(carry, packed):
        adj_now, acc_res, acc_pole = carry
        cot_row, prev_row, input_row = packed
        adj_now = cot_row[None, :] + decay_step * adj_now
        state_now = decay_step * prev_row + input_row[None, :]
        acc_res = acc_res + cot_row[None, :] * state_now
        acc_pole = acc_pole + adj_now * prev_row
        return ((adj_now, acc_res, acc_pole), lax.optimization_barrier(jnp.sum(residues_blk * adj_now, axis=0)))
    start = (zero_state, zero_state, zero_state)
    finals, grad_rows = lax.scan(backward_step, start, (cotan_vals, prev_states, input_vals), reverse=True)
    return (grad_rows.astype(jnp.bfloat16), finals[1], finals[2])

def reference(inputs, cotangent, rate, residues):
    batch_count, seq_len, channels = inputs.shape
    mode_count = rate.shape[0]
    block_width = 512 if channels % 512 == 0 else channels
    block_count = channels // block_width
    rate_blocks = rate.reshape(mode_count, block_count, block_width).transpose(1, 0, 2)
    res_blocks = residues.reshape(mode_count, block_count, block_width).transpose(1, 0, 2)

    def one_sequence(packed):
        seq_in, seq_cot = packed
        in_blocks = seq_in.reshape(seq_len, block_count, block_width).transpose(1, 0, 2)
        cot_blocks = seq_cot.reshape(seq_len, block_count, block_width).transpose(1, 0, 2)
        grads, acc_res, acc_pole = lax.map(lambda item: channel_block(*item), (in_blocks, cot_blocks, rate_blocks, res_blocks))
        grad_seq = grads.transpose(1, 0, 2).reshape(seq_len, channels)
        acc_res = acc_res.transpose(1, 0, 2).reshape(mode_count, channels)
        acc_pole = acc_pole.transpose(1, 0, 2).reshape(mode_count, channels)
        return (grad_seq, acc_res, acc_pole)
    grad_inputs, res_terms, pole_terms = lax.map(one_sequence, (inputs, cotangent))
    grad_scale = 1.0 / math.sqrt(batch_count * seq_len)
    decay_step = jnp.exp(-rate)
    grad_residues = lax.optimization_barrier(jnp.sum(res_terms, axis=0)) * grad_scale
    grad_rate = -decay_step * residues * lax.optimization_barrier(jnp.sum(pole_terms, axis=0)) * grad_scale
    return (grad_inputs, grad_residues, grad_rate)
```

```python
import functools
import math

import jax
import jax.numpy as jnp
from jax import lax
from jax.experimental import pallas as pl
from jax.experimental.pallas import tpu as pltpu
from jax.sharding import PartitionSpec as P

LANES = 128
SUBS = 8
SPAN = 8
PARTS = 6
END, START, DEND, DSTART, RES, POLE = range(PARTS)
f32 = jnp.float32


def horner(values, point):
    value, slope, scaled = values[0], None, None
    for item in values[1:]:
        if slope is None:
            slope = value
        elif scaled is not None and slope is values[0]:
            slope = scaled + value
        else:
            slope = slope * point + value
        scaled = value * point
        value = scaled + item
    return value, slope


def spread(tiles, scratch, rows, stride):
    for place, tile in enumerate(tiles):
        scratch[pl.ds(place, rows, stride=stride), :] = tile


def summary_kernel(where, *refs, rows, modes, together):
    x_tiles, c_tiles, r_tiles = refs[:SUBS], refs[SUBS : 2 * SUBS], refs[2 * SUBS : 3 * SUBS]
    out, rate_out, xs, cs, kept = refs[3 * SUBS :]
    blocks = rows // SPAN
    for place in range(SUBS):
        xs[pl.ds(place, rows, stride=SUBS), :] = x_tiles[place][...].astype(f32)
        cs[pl.ds(place, rows, stride=SUBS), :] = c_tiles[place][...].astype(f32)
        rate_out[pl.ds(place, modes, stride=SUBS), :] = r_tiles[place][...]

    def row(ref, index):
        return ref[pl.ds(pl.multiple_of(index * SUBS, SUBS), SUBS), :]

    zero = jnp.zeros((SUBS, LANES), f32)

    def lag_step(block, sums):
        xv = [row(xs, block * SPAN + k) for k in range(SPAN)]
        cv = [row(cs, block * SPAN + k) for k in range(SPAN)]
        return tuple(
            sums[lag] + sum(cv[k] * xv[k - lag] for k in range(lag, SPAN)) for lag in range(SPAN)
        )

    lags = lax.fori_loop(0, blocks, lag_step, (zero,) * SPAN)
    for lag in range(SPAN):
        kept[pl.ds(2 * together * blocks * SUBS + lag * SUBS, SUBS), :] = lags[lag]

    def slot(mode, block, which):
        return pl.ds(pl.multiple_of(((mode * blocks + block) * 2 + which) * SUBS, SUBS), SUBS)

    def some_modes(group, carry):
        ids = [group * together + m for m in range(together)]
        rates = [row(rate_out, n) for n in ids]
        poles = [jnp.exp(-r) for r in rates]
        spans = [jnp.exp(-r * SPAN) for r in rates]
        slopes = [jnp.exp(-r * (SPAN - 1)) * SPAN for r in rates]

        def forward(block, state):
            xv = [row(xs, block * SPAN + k) for k in range(SPAN)]
            new = []
            for m in range(together):
                now, dnow = state[m]
                value, slope = horner(xv, poles[m])
                push = slope + slopes[m] * now
                kept[slot(m, block, 0), :] = now
                kept[slot(m, block, 1), :] = push
                new.append((now * spans[m] + value, dnow * spans[m] + push))
            return tuple(new)

        ends = lax.fori_loop(0, blocks, forward, ((zero, zero),) * together, unroll=2)

        def backward(index, state):
            block = blocks - 1 - index
            cv = [row(cs, block * SPAN + k) for k in reversed(range(SPAN))]
            new = []
            for m in range(together):
                now, dnow, first, second = state[m]
                value, slope = horner(cv, poles[m])
                entry = kept[slot(m, block, 0), :]
                push = kept[slot(m, block, 1), :]
                first = first + entry * value
                second = second + (entry * slope + now * push)
                new.append(
                    (
                        now * spans[m] + value,
                        dnow * spans[m] + (slope + slopes[m] * now),
                        first,
                        second,
                    )
                )
            return tuple(new)

        starts = lax.fori_loop(0, blocks, backward, ((zero,) * 4,) * together, unroll=2)
        lagged = [
            kept[pl.ds(2 * together * blocks * SUBS + lag * SUBS, SUBS), :]
            for lag in reversed(range(SPAN))
        ]
        for m in range(together):
            value, slope = horner(lagged, poles[m])
            first, second = starts[m][2:]
            results = (
                ends[m][0],
                starts[m][0],
                ends[m][1],
                starts[m][1],
                poles[m] * first + value,
                first + poles[m] * second + slope,
            )
            for part in range(PARTS):
                base = pl.multiple_of((part * modes + ids[m]) * SUBS, SUBS)
                out[pl.ds(base, SUBS), :] = results[part]
        return carry

    lax.fori_loop(0, modes // together, some_modes, 0)


def pair_tiles(chips, core):
    def tile_map(place):
        q, chip = place % 4, chips[place // 4]
        return lambda i, w: (0, 8 * q + 2 * (w[0] ^ chip) + (w[1] ^ core))

    return tile_map


def next_tiles(first):
    return lambda place: lambda i, w: (0, first + place)


def summaries(where, inputs, cotangent, rate, tile_map):
    rows, modes = inputs.shape[0], rate.shape[0]
    together = 4

    tiles = lambda height: [pl.BlockSpec((height, LANES), tile_map(s)) for s in range(SUBS)]
    return pl.pallas_call(
        functools.partial(summary_kernel, rows=rows, modes=modes, together=together),
        grid_spec=pltpu.PrefetchScalarGridSpec(
            num_scalar_prefetch=1,
            grid=(1,),
            in_specs=tiles(rows) + tiles(rows) + tiles(modes),
            out_specs=[
                pl.BlockSpec((PARTS * modes * SUBS, LANES), lambda i, w: (0, 0)),
                pl.BlockSpec((modes * SUBS, LANES), lambda i, w: (0, 0)),
            ],
            scratch_shapes=[
                pltpu.VMEM((rows * SUBS, LANES), f32),
                pltpu.VMEM((rows * SUBS, LANES), f32),
                pltpu.VMEM(((2 * together * rows // SPAN + SPAN) * SUBS, LANES), f32),
            ],
        ),
        out_shape=[
            jax.ShapeDtypeStruct((PARTS * modes * SUBS, LANES), f32),
            jax.ShapeDtypeStruct((modes * SUBS, LANES), f32),
        ],
        name="summaries",
    )(where, *([inputs] * SUBS), *([cotangent] * SUBS), *([rate] * SUBS))


def joined(one, two, pole, power, slope):
    cross = one[END] * two[START]
    return (
        power * one[END] + two[END],
        one[START] + power * two[START],
        slope * one[END] + power * one[DEND] + two[DEND],
        one[DSTART] + slope * two[START] + power * two[DSTART],
        one[RES] + two[RES] + pole * cross,
        one[POLE] + two[POLE] + cross + pole * (one[DEND] * two[START] + one[END] * two[DSTART]),
    )


def pair_kernel(where, own, other, rates, send0, send1, hold0, hold1, *, rows, modes):
    def body(one, two):
        for n in range(modes):
            r = rates[pl.ds(n * SUBS, SUBS), :]
            power = jnp.exp(-r * rows)
            read = lambda ref: [ref[pl.ds((a * modes + n) * SUBS, SUBS), :] for a in range(PARTS)]
            first, second = read(one), read(two)
            result = joined(
                first, second, jnp.exp(-r), power, jnp.exp(-r * (rows - 1)) * float(rows)
            )
            for a in range(PARTS):
                send0[pl.ds((a * modes + n) * 4, 4), :] = result[a][:4]
                send1[pl.ds((a * modes + n) * 4, 4), :] = result[a][4:]
            for a, item in enumerate((second[START], power)):
                hold0[pl.ds((a * modes + n) * 4, 4), :] = item[:4]
                hold1[pl.ds((a * modes + n) * 4, 4), :] = item[4:]

    @pl.when(where[1] == 0)
    def _():
        body(own, other)

    @pl.when(where[1] != 0)
    def _():
        body(other, own)


def paired(where, own, other, rates, rows, modes):
    whole = lambda: pl.BlockSpec(memory_space=pltpu.VMEM)
    shape = lambda count: jax.ShapeDtypeStruct((count * modes * 4, LANES), f32)
    return pl.pallas_call(
        functools.partial(pair_kernel, rows=rows, modes=modes),
        in_specs=[pl.BlockSpec(memory_space=pltpu.SMEM), whole(), whole(), whole()],
        out_specs=[whole() for _ in range(4)],
        out_shape=[shape(PARTS), shape(PARTS), shape(2), shape(2)],
        name="paired",
    )(where, own, other, rates)


def chain_kernel(where, *refs, rows, modes, scale):
    pieces, r_tiles, res_tiles = refs[:4], refs[4:8], refs[8:12]
    backs, terms = refs[12:16], refs[16:20]
    ordered, adjoints, small, owned = refs[20:]
    size = modes * 4
    for j in range(4):
        ordered[where[0] ^ j] = pieces[j][...]
    for q in range(4):
        small[0, pl.ds(q, modes, stride=4), :] = r_tiles[q][...]
        small[1, pl.ds(q, modes, stride=4), :] = res_tiles[q][...]
    r = small[0]
    pole = jnp.exp(-r)
    power = jnp.exp(-r * rows)
    slope = jnp.exp(-r * (rows - 1)) * float(rows)
    read = lambda c, a: ordered[c, pl.ds(a * size, size), :]
    now, dnow = read(0, END), read(0, DEND)
    sum_res, sum_pole = read(0, RES), read(0, POLE)
    for c in range(1, 4):
        start, dstart = read(c, START), read(c, DSTART)
        cross = now * start
        sum_res = sum_res + read(c, RES) + pole * cross
        sum_pole = sum_pole + read(c, POLE) + cross + pole * (dnow * start + now * dstart)
        if c < 3:
            now, dnow = (
                power * now + read(c, END),
                slope * now + power * dnow + read(c, DEND),
            )
    back = jnp.zeros((size, LANES), f32)
    adjoints[3] = back
    for c in range(2, -1, -1):
        back = read(c + 1, START) + power * back
        adjoints[c] = back
    for j in range(4):
        backs[j][...] = adjoints[where[0] ^ j]
    owned[pl.ds(0, size), :] = sum_res * scale
    owned[pl.ds(size, size), :] = sum_pole * (-pole * small[1]) * scale
    for j in range(4):
        q = (where[2] + j) % 4
        for a in range(2):
            terms[j][pl.ds(a * modes, modes), :] = owned[pl.ds(a * size + q, modes, stride=4), :]


def chained(where, pieces, rate, residues, rows, scale):
    modes = rate.shape[0]

    def tile_map(q):
        return lambda i, w: (0, 8 * q + 2 * w[0] + w[1])

    whole = lambda height: pl.BlockSpec((height, LANES), lambda i, w: (0, 0))
    tiles = lambda: [pl.BlockSpec((modes, LANES), tile_map(q)) for q in range(4)]
    outs = pl.pallas_call(
        functools.partial(chain_kernel, rows=rows, modes=modes, scale=scale),
        grid_spec=pltpu.PrefetchScalarGridSpec(
            num_scalar_prefetch=1,
            grid=(1,),
            in_specs=[whole(PARTS * modes * 4) for _ in range(4)] + tiles() + tiles(),
            out_specs=[whole(modes * 4) for _ in range(4)] + [whole(2 * modes) for _ in range(4)],
            scratch_shapes=[
                pltpu.VMEM((4, PARTS * modes * 4, LANES), f32),
                pltpu.VMEM((4, modes * 4, LANES), f32),
                pltpu.VMEM((2, modes * 4, LANES), f32),
                pltpu.VMEM((2 * modes * 4, LANES), f32),
            ],
        ),
        out_shape=[jax.ShapeDtypeStruct((modes * 4, LANES), f32) for _ in range(4)]
        + [jax.ShapeDtypeStruct((2 * modes, LANES), f32) for _ in range(4)],
        name="chained",
    )(where, *pieces, *([rate] * 4), *([residues] * 4))
    return outs[:4], outs[4:]


def entry_kernel(where, *refs, modes):
    backs, holds, mine, theirs = refs[:4], refs[4:8], refs[8], refs[9]
    size = modes * 4

    def body(late, early):
        for j in range(4):
            back = backs[j][...]
            late[pl.ds(j * size, size), :] = back
            early[pl.ds(j * size, size), :] = holds[j][:size, :] + holds[j][size:, :] * back

    @pl.when(where[1] == 0)
    def _():
        body(theirs, mine)

    @pl.when(where[1] != 0)
    def _():
        body(mine, theirs)


def entries(where, backs, holds, modes):
    whole = lambda: pl.BlockSpec(memory_space=pltpu.VMEM)
    shape = jax.ShapeDtypeStruct((4 * modes * 4, LANES), f32)
    return pl.pallas_call(
        functools.partial(entry_kernel, modes=modes),
        in_specs=[pl.BlockSpec(memory_space=pltpu.SMEM)] + [whole() for _ in range(8)],
        out_specs=[whole(), whole()],
        out_shape=[shape, shape],
        name="entries",
    )(where, *backs, *holds)


def input_kernel(where, cot, rate, res, *refs, rows, modes, together):
    q = pl.program_id(0)
    size = modes * 4
    given, (out, cs, ys, ps, rs, ads) = refs[:-6], refs[-6:]
    for i in range(SUBS):
        lanes = pl.ds(i * LANES, LANES)
        cs[pl.ds(i, rows, stride=SUBS), :] = cot[:, lanes].astype(f32)
        ps[pl.ds(i, modes, stride=SUBS), :] = jnp.exp(-rate[:, lanes])
        rs[pl.ds(i, modes, stride=SUBS), :] = res[:, lanes]
    if len(given) == 1:
        spread([given[0][:, pl.ds(i * LANES, LANES)] for i in range(SUBS)], ads, modes, SUBS)
    for j in range(4 if len(given) == 2 else 0):
        for core, source in enumerate(given):
            i = 2 * (where[0] ^ j) + (where[1] ^ core)
            ads[pl.ds(i, modes, stride=SUBS), :] = source[pl.ds(j * size + q, modes, stride=4), :]

    for group in range(modes // together):
        at = [pl.ds((group * together + m) * SUBS, SUBS) for m in range(together)]
        poles = [ps[a, :] for a in at]
        weights = [rs[a, :] for a in at]

        def step(index, adjoint):
            here = pl.ds(pl.multiple_of((rows - 1 - index) * SUBS, SUBS), SUBS)
            value = cs[here, :]
            adjoint = tuple(a * p + value for a, p in zip(adjoint, poles))
            terms = [a * w for a, w in zip(adjoint, weights)]
            while len(terms) > 1:
                terms = [a + b for a, b in zip(terms[::2], terms[1::2])]
            ys[here, :] = terms[0] if group == 0 else ys[here, :] + terms[0]
            return adjoint

        lax.fori_loop(0, rows, step, tuple(ads[a, :] for a in at), unroll=4)
    for i in range(SUBS):
        out[:, pl.ds(i * LANES, LANES)] = ys[pl.ds(i, rows, stride=SUBS), :].astype(out.dtype)


def input_gradients(where, cotangent, rate, residues, *given):
    rows, channels = cotangent.shape
    modes = rate.shape[0]
    width = SUBS * LANES
    block = lambda height: pl.BlockSpec((height, width), lambda i, w: (0, i))
    whole = lambda: pl.BlockSpec((16 * modes, LANES), lambda i, w: (0, 0))
    scratch = lambda height: pltpu.VMEM((height * SUBS, LANES), f32)
    return pl.pallas_call(
        functools.partial(input_kernel, rows=rows, modes=modes, together=8),
        grid_spec=pltpu.PrefetchScalarGridSpec(
            num_scalar_prefetch=1,
            grid=(channels // width,),
            in_specs=[block(rows), block(modes), block(modes)]
            + ([block(modes)] if len(given) == 1 else [whole(), whole()]),
            out_specs=block(rows),
            scratch_shapes=[scratch(rows), scratch(rows), scratch(modes), scratch(modes), scratch(modes)],
        ),
        out_shape=jax.ShapeDtypeStruct((rows, channels), cotangent.dtype),
        name="input_gradients",
    )(where, cotangent, rate, residues, *given)


def place_kernel(where, *refs, modes):
    pieces, out_res, out_rate = refs[:4], refs[4], refs[5]
    for j in range(4):
        for core in range(2):
            i = 2 * (where[0] ^ j) + (where[1] ^ core)
            lanes = pl.ds(pl.multiple_of(i * LANES, LANES), LANES)
            out_res[:, lanes] = pieces[j][pl.ds(core * 2 * modes, modes), :]
            out_rate[:, lanes] = pieces[j][pl.ds((core * 2 + 1) * modes, modes), :]


def placed(where, pieces, modes):
    whole = lambda: pl.BlockSpec(memory_space=pltpu.VMEM)
    shape = jax.ShapeDtypeStruct((modes, SUBS * LANES), f32)
    return pl.pallas_call(
        functools.partial(place_kernel, modes=modes),
        in_specs=[pl.BlockSpec(memory_space=pltpu.SMEM)] + [whole() for _ in range(4)],
        out_specs=[whole(), whole()],
        out_shape=[shape, shape],
        name="placed",
    )(where, *pieces)


def crossed(value, distance):
    return lax.ppermute(value, "context", [(i, i ^ distance) for i in range(8)])


def shifted(value, distance):
    return lax.ppermute(value, "dp", [(i, (i + distance) % 4) for i in range(4)])


def four_by_eight(inputs, cotangent, rate, residues):
    x, c = inputs[0], cotangent[0]
    rows, modes = x.shape[0], rate.shape[0]
    context = lax.axis_index("context")
    where = jnp.stack([context // 2, context % 2, lax.axis_index("dp")]).astype(jnp.int32)
    sends, holds = {}, {}
    for chips in ((3, 2), (1, 0)):
        away, _ = summaries(where, x, c, rate, pair_tiles(chips, 1))
        other = crossed(away, 1)
        own, rates = summaries(where, x, c, rate, pair_tiles(chips, 0))
        sends[chips[0]], sends[chips[1]], holds[chips[0]], holds[chips[1]] = paired(
            where, own, other, rates, rows, modes
        )
    pieces = [sends[0]] + [crossed(sends[j], 2 * j) for j in (1, 2, 3)]
    scale = 1.0 / math.sqrt(4 * rows * 8)
    backs, terms = chained(where, pieces, rate, residues, 2 * rows, scale)
    shares = [terms[0]] + [shifted(terms[j], j) for j in (1, 2, 3)]
    backs = [backs[0]] + [crossed(backs[j], 2 * j) for j in (1, 2, 3)]
    mine, theirs = entries(where, backs, [holds[j] for j in range(4)], modes)
    theirs = crossed(theirs, 1)
    grad_inputs = input_gradients(where, c, rate, residues, mine, theirs)
    total = shares[0] + shares[1] + shares[2] + shares[3]
    both = jnp.concatenate([total, crossed(total, 1)])
    grad_residues, grad_rate = placed(
        where, [both] + [crossed(both, 2 * j) for j in (1, 2, 3)], modes
    )
    return (grad_inputs[None], grad_residues, grad_rate)


def any_mesh(inputs, cotangent, rate, residues):
    x, c = inputs[0], cotangent[0]
    rows, channels, modes = x.shape[0], x.shape[1], rate.shape[0]
    count, mine = lax.axis_size("context"), lax.axis_index("context")
    where = jnp.zeros((3,), jnp.int32)
    blocks = [
        summaries(where, x, c, rate, next_tiles(first))[0]
        for first in range(0, channels // LANES, SUBS)
    ]
    local = jnp.stack(blocks).reshape(-1, PARTS, modes, SUBS * LANES)
    local = jnp.moveaxis(local, 0, 2).reshape(PARTS, modes, channels)
    slabs = lax.all_gather(local, "context")
    pole, power = jnp.exp(-rate), jnp.exp(-rate * rows)
    slope = jnp.exp(-rate * (rows - 1)) * rows
    total = tuple(slabs[0])
    for place in range(1, count):
        total = joined(total, slabs[place], pole, power, slope)
    zero = jnp.zeros_like(pole)

    def behind(index, entry):
        place = count - 1 - index
        return jnp.where(place > mine, slabs[place, START] + power * entry, entry)

    entry = lax.fori_loop(0, count, behind, zero)
    grad_inputs = input_gradients(where, c, rate, residues, entry)
    scale = 1.0 / math.sqrt(lax.axis_size("dp") * rows * count)
    terms = jnp.stack([total[RES], total[POLE] * (-pole * residues)]) * scale
    owned = lax.psum_scatter(terms, "dp", scatter_dimension=2, tiled=True)
    return (grad_inputs[None], owned[0], owned[1])


def solution(mesh):
    tuned = mesh.shape["dp"] == 4 and mesh.shape["context"] == 8
    in_specs = (P("dp", "context", None), P("dp", "context", None), P(), P())
    out_specs = (P("dp", "context", None), P(None, "dp"), P(None, "dp"))
    return jax.shard_map(
        four_by_eight if tuned else any_mesh, mesh=mesh, in_specs=in_specs, out_specs=out_specs, check_vma=False
    )
```

```python
import functools
import math

import jax
import jax.numpy as jnp
from jax import lax
from jax.experimental import pallas as pl
from jax.experimental.pallas import tpu as pltpu
from jax.sharding import PartitionSpec as P

LANES = 128
SUBS = 8
SPAN = 8
PARTS = 6
END, START, DEND, DSTART, RES, POLE = range(PARTS)
f32 = jnp.float32


def here(value):
    return pltpu.with_memory_space_constraint(value, pltpu.VMEM)


def vmem():
    return pl.BlockSpec(memory_space=pltpu.VMEM)


def position():
    context = lax.axis_index("context")
    return context // 2, context % 2, lax.axis_index("dp")


def room(megabytes):
    return pltpu.CompilerParams(vmem_limit_bytes=megabytes << 20)


def work(operations, touched):
    return pl.CostEstimate(flops=operations, transcendentals=0, bytes_accessed=touched)


def local_call(kernel, name, shapes, operands, scratch=(), megabytes=2, cost=None):
    return pl.pallas_call(
        kernel,
        in_specs=[vmem() for _ in operands],
        out_specs=[vmem() for _ in shapes],
        out_shape=[pltpu.VMEM(shape, f32) for shape in shapes],
        scratch_shapes=[pltpu.VMEM(shape, f32) for shape in scratch],
        compiler_params=room(megabytes),
        cost_estimate=cost,
        name=name,
    )(*[here(item) for item in operands])


def horner(values, point):
    value, slope, scaled = values[0], None, None
    for item in values[1:]:
        if slope is None:
            slope = value
        elif scaled is not None and slope is values[0]:
            slope = scaled + value
        else:
            slope = slope * point + value
        scaled = value * point
        value = scaled + item
    return value, slope


def spread(tiles, scratch, rows, stride):
    for place, tile in enumerate(tiles):
        scratch[pl.ds(place, rows, stride=stride), :] = tile


def summary_kernel(x, c, rate, *refs, **static):
    summarize(x, c, rate, *refs[-5:], **static)


def first_kernel(x, c, rate, res, out, rate_out, x_in, c_in, rate_in, res_in, xs, cs, kept, done, **static):
    chip, _, _ = position()
    width = 4 * LANES
    copies = []
    for pair in range(2):
        for q in range(4):
            start = 8 * LANES * q + width * ((chip // 2) ^ (1 - pair))
            lanes = pl.ds(pl.multiple_of(start, width), width)
            copies += [(ref.at[:, lanes], into.at[:, lanes]) for ref, into in ((x, x_in), (c, c_in))]
        if pair == 0:
            copies.append((rate, rate_in))
    copies.append((res, res_in))
    copies = [
        pltpu.make_async_copy(source, into, done.at[place])
        for place, (source, into) in enumerate(copies)
    ]
    for copy in copies:
        copy.start()
    for copy in copies[:9]:
        copy.wait()
    summarize(x_in, c_in, rate_in, out, rate_out, xs, cs, kept, **static)
    for copy in copies[9:]:
        copy.wait()


def summarize(x, c, rate, out, rate_out, xs, cs, kept, *, tile_of, rows, modes, together):
    blocks = rows // SPAN
    for place in range(SUBS):
        lanes = pl.ds(pl.multiple_of(tile_of(place) * LANES, LANES), LANES)
        xs[pl.ds(place, rows, stride=SUBS), :] = x[:, lanes].astype(f32)
        cs[pl.ds(place, rows, stride=SUBS), :] = c[:, lanes].astype(f32)
        rate_out[pl.ds(place, modes, stride=SUBS), :] = rate[:, lanes]

    def row(ref, index):
        return ref[pl.ds(pl.multiple_of(index * SUBS, SUBS), SUBS), :]

    zero = jnp.zeros((SUBS, LANES), f32)

    def lag_step(block, sums):
        xv = [row(xs, block * SPAN + k) for k in range(SPAN)]
        cv = [row(cs, block * SPAN + k) for k in range(SPAN)]
        return tuple(
            sums[lag] + sum(cv[k] * xv[k - lag] for k in range(lag, SPAN)) for lag in range(SPAN)
        )

    lags = lax.fori_loop(0, blocks, lag_step, (zero,) * SPAN)
    for lag in range(SPAN):
        kept[pl.ds(2 * together * blocks * SUBS + lag * SUBS, SUBS), :] = lags[lag]

    def slot(mode, block, which):
        return pl.ds(pl.multiple_of(((mode * blocks + block) * 2 + which) * SUBS, SUBS), SUBS)

    def some_modes(group, carry):
        ids = [group * together + m for m in range(together)]
        rates = [row(rate_out, n) for n in ids]
        poles = [jnp.exp(-r) for r in rates]
        spans = [jnp.exp(-r * SPAN) for r in rates]
        slopes = [jnp.exp(-r * (SPAN - 1)) * SPAN for r in rates]

        def forward(block, state):
            xv = [row(xs, block * SPAN + k) for k in range(SPAN)]
            new = []
            for m in range(together):
                now, dnow = state[m]
                value, slope = horner(xv, poles[m])
                push = slope + slopes[m] * now
                kept[slot(m, block, 0), :] = now
                kept[slot(m, block, 1), :] = push
                new.append((now * spans[m] + value, dnow * spans[m] + push))
            return tuple(new)

        ends = lax.fori_loop(0, blocks, forward, ((zero, zero),) * together, unroll=True)

        def backward(index, state):
            block = blocks - 1 - index
            cv = [row(cs, block * SPAN + k) for k in reversed(range(SPAN))]
            new = []
            for m in range(together):
                now, dnow, first, second = state[m]
                value, slope = horner(cv, poles[m])
                entry = kept[slot(m, block, 0), :]
                push = kept[slot(m, block, 1), :]
                first = first + entry * value
                second = second + (entry * slope + now * push)
                new.append(
                    (
                        now * spans[m] + value,
                        dnow * spans[m] + (slope + slopes[m] * now),
                        first,
                        second,
                    )
                )
            return tuple(new)

        starts = lax.fori_loop(0, blocks, backward, ((zero,) * 4,) * together, unroll=True)
        lagged = [
            kept[pl.ds(2 * together * blocks * SUBS + lag * SUBS, SUBS), :]
            for lag in reversed(range(SPAN))
        ]
        for m in range(together):
            value, slope = horner(lagged, poles[m])
            first, second = starts[m][2:]
            results = (
                ends[m][0],
                starts[m][0],
                ends[m][1],
                starts[m][1],
                poles[m] * first + value,
                first + poles[m] * second + slope,
            )
            for part in range(PARTS):
                base = pl.multiple_of((part * modes + ids[m]) * SUBS, SUBS)
                out[pl.ds(base, SUBS), :] = results[part]
        return carry

    lax.fori_loop(0, modes // together, some_modes, 0)


def pair_tiles(chips, core):
    def tile_of(place):
        chip, half, _ = position()
        return 8 * (place % 4) + 2 * (chip ^ chips[place // 4]) + (half ^ core)

    return tile_of


def next_tiles(first):
    return lambda place: first + place


def summary_parts(rows, modes, tile_of):
    together = 2
    kept = (2 * together * rows // SPAN + SPAN) * SUBS
    static = dict(tile_of=tile_of, rows=rows, modes=modes, together=together)
    shapes = [(PARTS * modes * SUBS, LANES), (modes * SUBS, LANES)]
    cost = work(10 * rows * modes * SUBS * LANES, 4 << 20)
    return static, shapes, [(rows * SUBS, LANES), (rows * SUBS, LANES), (kept, LANES)], cost


def summaries(inputs, cotangent, rate, tile_of, after=()):
    static, shapes, scratch, cost = summary_parts(inputs.shape[0], rate.shape[0], tile_of)
    kernel = functools.partial(summary_kernel, **static)
    return local_call(
        kernel, "summaries", shapes, [inputs, cotangent, rate, *after], scratch, 4, cost
    )


def first_summaries(inputs, cotangent, rate, residues, tile_of):
    static, shapes, scratch, cost = summary_parts(inputs.shape[0], rate.shape[0], tile_of)
    operands = (inputs, cotangent, rate, residues)
    return pl.pallas_call(
        functools.partial(first_kernel, **static),
        in_specs=[pl.BlockSpec(memory_space=pltpu.HBM) for _ in operands],
        out_specs=[vmem() for _ in range(6)],
        out_shape=[pltpu.VMEM(shape, f32) for shape in shapes]
        + [pltpu.VMEM(item.shape, item.dtype) for item in operands],
        scratch_shapes=[pltpu.VMEM(shape, f32) for shape in scratch]
        + [pltpu.SemaphoreType.DMA((18,))],
        compiler_params=room(4),
        cost_estimate=cost,
        name="first_summaries",
    )(*[pltpu.with_memory_space_constraint(item, pltpu.HBM) for item in operands])


def joined(one, two, pole, power, slope):
    cross = one[END] * two[START]
    return (
        power * one[END] + two[END],
        one[START] + power * two[START],
        slope * one[END] + power * one[DEND] + two[DEND],
        one[DSTART] + slope * two[START] + power * two[DSTART],
        one[RES] + two[RES] + pole * cross,
        one[POLE] + two[POLE] + cross + pole * (one[DEND] * two[START] + one[END] * two[DSTART]),
    )


def pair_kernel(own, other, rates, send0, send1, hold0, hold1, *, rows, modes):
    def body(one, two):
        for n in range(modes):
            r = rates[pl.ds(n * SUBS, SUBS), :]
            power = jnp.exp(-r * rows)
            read = lambda ref: [ref[pl.ds((a * modes + n) * SUBS, SUBS), :] for a in range(PARTS)]
            first, second = read(one), read(two)
            result = joined(
                first, second, jnp.exp(-r), power, jnp.exp(-r * (rows - 1)) * float(rows)
            )
            for a in range(PARTS):
                send0[pl.ds((a * modes + n) * 4, 4), :] = result[a][:4]
                send1[pl.ds((a * modes + n) * 4, 4), :] = result[a][4:]
            for a, item in enumerate((second[START], power)):
                hold0[pl.ds((a * modes + n) * 4, 4), :] = item[:4]
                hold1[pl.ds((a * modes + n) * 4, 4), :] = item[4:]

    core = position()[1]

    @pl.when(core == 0)
    def _():
        body(own, other)

    @pl.when(core != 0)
    def _():
        body(other, own)


def paired(own, other, rates, rows, modes):
    return local_call(
        functools.partial(pair_kernel, rows=rows, modes=modes),
        "paired",
        [(count * modes * 4, LANES) for count in (PARTS, PARTS, 2, 2)],
        [own, other, rates],
    )


def chain_kernel(*refs, rows, modes, scale):
    pieces, (rate, residues) = refs[:4], refs[4:6]
    backs, terms = refs[6:10], refs[10:14]
    ordered, adjoints, small, owned = refs[14:]
    chip, core, depth = position()
    size = modes * 4
    for j in range(4):
        ordered[chip ^ j] = pieces[j][...]
    for q in range(4):
        lanes = pl.ds(pl.multiple_of((8 * q + 2 * chip + core) * LANES, LANES), LANES)
        small[0, pl.ds(q, modes, stride=4), :] = rate[:, lanes]
        small[1, pl.ds(q, modes, stride=4), :] = residues[:, lanes]
    r = small[0]
    pole = jnp.exp(-r)
    power = jnp.exp(-r * rows)
    slope = jnp.exp(-r * (rows - 1)) * float(rows)
    read = lambda c, a: ordered[c, pl.ds(a * size, size), :]
    now, dnow = read(0, END), read(0, DEND)
    sum_res, sum_pole = read(0, RES), read(0, POLE)
    for c in range(1, 4):
        start, dstart = read(c, START), read(c, DSTART)
        cross = now * start
        sum_res = sum_res + read(c, RES) + pole * cross
        sum_pole = sum_pole + read(c, POLE) + cross + pole * (dnow * start + now * dstart)
        if c < 3:
            now, dnow = (
                power * now + read(c, END),
                slope * now + power * dnow + read(c, DEND),
            )
    back = jnp.zeros((size, LANES), f32)
    adjoints[3] = back
    for c in range(2, -1, -1):
        back = read(c + 1, START) + power * back
        adjoints[c] = back
    for j in range(4):
        backs[j][...] = adjoints[chip ^ j]
    owned[pl.ds(0, size), :] = sum_res * scale
    owned[pl.ds(size, size), :] = sum_pole * (-pole * small[1]) * scale
    for j in range(4):
        q = (depth + j) % 4
        for a in range(2):
            terms[j][pl.ds(a * modes, modes), :] = owned[pl.ds(a * size + q, modes, stride=4), :]


def chained(pieces, rate, residues, rows, scale):
    modes = rate.shape[0]
    size = modes * 4
    outs = local_call(
        functools.partial(chain_kernel, rows=rows, modes=modes, scale=scale),
        "chained",
        [(size, LANES)] * 4 + [(2 * modes, LANES)] * 4,
        [*pieces, rate, residues],
        [(4, PARTS * size, LANES), (4, size, LANES), (2, size, LANES), (2 * size, LANES)],
    )
    return outs[:4], outs[4:]


def entry_kernel(*refs, modes):
    backs, holds, mine, theirs = refs[:4], refs[4:8], refs[8], refs[9]
    size = modes * 4

    def body(late, early):
        for j in range(4):
            back = backs[j][...]
            late[pl.ds(j * size, size), :] = back
            early[pl.ds(j * size, size), :] = holds[j][:size, :] + holds[j][size:, :] * back

    core = position()[1]

    @pl.when(core == 0)
    def _():
        body(theirs, mine)

    @pl.when(core != 0)
    def _():
        body(mine, theirs)


def entries(backs, holds, modes):
    return local_call(
        functools.partial(entry_kernel, modes=modes),
        "entries",
        [(4 * modes * 4, LANES)] * 2,
        [*backs, *holds],
    )


def input_kernel(cot, rate, res, *refs, rows, modes, together):
    given, (out, cs, ys, ps, rs, ads, sent, done) = refs[:-8], refs[-8:]
    chip, half, _ = position() if len(given) == 2 else (None,) * 3
    width = SUBS * LANES

    def copy(q):
        lanes = pl.ds(pl.multiple_of(q * width, width), width)
        return pltpu.make_async_copy(sent.at[q], out.at[:, lanes], done.at[q])

    def one_block(q, carry):
        block_of_inputs(q, cot, rate, res, given, (chip, half), sent, (cs, ys, ps, rs, ads), rows, modes, together)
        copy(q).start()
        return carry

    count = cot.shape[1] // width
    lax.fori_loop(0, count, one_block, 0)
    for q in range(count):
        copy(q).wait()


def block_of_inputs(q, cot, rate, res, given, place, sent, scratch, rows, modes, together):
    cs, ys, ps, rs, ads = scratch
    size = modes * 4

    def tile(i):
        return pl.ds(pl.multiple_of((q * SUBS + i) * LANES, LANES), LANES)

    for i in range(SUBS):
        lanes = tile(i)
        cs[pl.ds(i, rows, stride=SUBS), :] = cot[:, lanes].astype(f32)
        ps[pl.ds(i, modes, stride=SUBS), :] = jnp.exp(-rate[:, lanes])
        rs[pl.ds(i, modes, stride=SUBS), :] = res[:, lanes]
    if len(given) == 1:
        spread([given[0][:, tile(i)] for i in range(SUBS)], ads, modes, SUBS)
    for j in range(4 if len(given) == 2 else 0):
        for core, source in enumerate(given):
            i = 2 * (place[0] ^ j) + (place[1] ^ core)
            ads[pl.ds(i, modes, stride=SUBS), :] = source[pl.ds(j * size + q, modes, stride=4), :]

    for group in range(modes // together):
        at = [pl.ds((group * together + m) * SUBS, SUBS) for m in range(together)]
        poles = [ps[a, :] for a in at]
        weights = [rs[a, :] for a in at]

        def step(index, adjoint):
            now = pl.ds(pl.multiple_of((rows - 1 - index) * SUBS, SUBS), SUBS)
            value = cs[now, :]
            adjoint = tuple(a * p + value for a, p in zip(adjoint, poles))
            terms = [a * w for a, w in zip(adjoint, weights)]
            while len(terms) > 1:
                terms = [a + b for a, b in zip(terms[::2], terms[1::2])]
            ys[now, :] = terms[0] if group == 0 else ys[now, :] + terms[0]
            return adjoint

        lax.fori_loop(0, rows, step, tuple(ads[a, :] for a in at), unroll=4)
    for i in range(SUBS):
        sent[q, :, pl.ds(i * LANES, LANES)] = ys[pl.ds(i, rows, stride=SUBS), :].astype(sent.dtype)


def input_gradients(cotangent, rate, residues, *given):
    rows, channels = cotangent.shape
    modes = rate.shape[0]
    width = SUBS * LANES
    scratch = lambda height: pltpu.VMEM((height * SUBS, LANES), f32)
    operands = (cotangent, rate, residues, *given)
    return pl.pallas_call(
        functools.partial(input_kernel, rows=rows, modes=modes, together=8),
        in_specs=[vmem() for _ in operands],
        out_specs=pl.BlockSpec(memory_space=pl.ANY),
        out_shape=jax.ShapeDtypeStruct((rows, channels), cotangent.dtype),
        scratch_shapes=[
            scratch(rows),
            scratch(rows),
            scratch(modes),
            scratch(modes),
            scratch(modes),
            pltpu.VMEM((channels // width, rows, width), cotangent.dtype),
            pltpu.SemaphoreType.DMA((channels // width,)),
        ],
        compiler_params=room(5),
        cost_estimate=pl.CostEstimate(
            flops=4 * rows * channels * modes,
            transcendentals=modes * channels,
            bytes_accessed=2 * rows * channels,
        ),
        name="input_gradients",
    )(*[here(item) for item in operands])


def place_kernel(*refs, modes):
    pieces, (out_res, out_rate) = refs[:4], refs[-2:]
    chip, half, _ = position()
    for j in range(4):
        for core in range(2):
            i = 2 * (chip ^ j) + (half ^ core)
            lanes = pl.ds(pl.multiple_of(i * LANES, LANES), LANES)
            out_res[:, lanes] = pieces[j][pl.ds(core * 2 * modes, modes), :]
            out_rate[:, lanes] = pieces[j][pl.ds((core * 2 + 1) * modes, modes), :]


def placed(pieces, modes, after):
    shape = jax.ShapeDtypeStruct((modes, SUBS * LANES), f32)
    return pl.pallas_call(
        functools.partial(place_kernel, modes=modes),
        in_specs=[vmem() for _ in pieces] + [pl.BlockSpec(memory_space=pltpu.HBM)],
        out_specs=[vmem(), vmem()],
        out_shape=[shape, shape],
        compiler_params=room(2),
        name="placed",
    )(
        *[here(item) for item in pieces],
        pltpu.with_memory_space_constraint(after, pltpu.HBM),
    )


def crossed(value, distance):
    return lax.ppermute(value, "context", [(i, i ^ distance) for i in range(8)])


def shifted(value, distance):
    return lax.ppermute(value, "dp", [(i, (i + distance) % 4) for i in range(4)])


def four_by_eight(inputs, cotangent, rate, residues):
    x, c = inputs[0], cotangent[0]
    rows, modes = x.shape[0], rate.shape[0]
    sends, holds, after = {}, {}, ()
    for chips in ((3, 2), (1, 0)):
        if after:
            away, _ = summaries(x, c, rate, pair_tiles(chips, 1), after)
        else:
            away, _, x, c, rate, residues = first_summaries(
                x, c, rate, residues, pair_tiles(chips, 1)
            )
        other = crossed(away, 1)
        own, rates = summaries(x, c, rate, pair_tiles(chips, 0))
        sends[chips[0]], sends[chips[1]], holds[chips[0]], holds[chips[1]] = paired(
            own, other, rates, rows, modes
        )
        after = (holds[chips[0]],)
    pieces = [sends[0]] + [crossed(sends[j], 2 * j) for j in (1, 2, 3)]
    scale = 1.0 / math.sqrt(4 * rows * 8)
    backs, terms = chained(pieces, rate, residues, 2 * rows, scale)
    shares = [terms[0]] + [shifted(terms[j], j) for j in (1, 2, 3)]
    backs = [backs[0]] + [crossed(backs[j], 2 * j) for j in (1, 2, 3)]
    mine, theirs = entries(backs, [holds[j] for j in range(4)], modes)
    theirs = crossed(theirs, 1)
    grad_inputs = input_gradients(c, rate, residues, mine, theirs)
    total = shares[0] + shares[1] + shares[2] + shares[3]
    both = jnp.concatenate([total, crossed(total, 1)])
    gathered = [both] + [crossed(both, 2 * j) for j in (1, 2, 3)]
    grad_residues, grad_rate = placed(gathered, modes, grad_inputs)
    return (grad_inputs[None], grad_residues, grad_rate)


def any_mesh(inputs, cotangent, rate, residues):
    x, c = inputs[0], cotangent[0]
    rows, channels, modes = x.shape[0], x.shape[1], rate.shape[0]
    count, mine = lax.axis_size("context"), lax.axis_index("context")
    blocks = [
        summaries(x, c, rate, next_tiles(first))[0]
        for first in range(0, channels // LANES, SUBS)
    ]
    local = jnp.stack(blocks).reshape(-1, PARTS, modes, SUBS * LANES)
    local = jnp.moveaxis(local, 0, 2).reshape(PARTS, modes, channels)
    slabs = lax.all_gather(local, "context")
    pole, power = jnp.exp(-rate), jnp.exp(-rate * rows)
    slope = jnp.exp(-rate * (rows - 1)) * rows
    total = tuple(slabs[0])
    for place in range(1, count):
        total = joined(total, slabs[place], pole, power, slope)
    zero = jnp.zeros_like(pole)

    def behind(index, entry):
        place = count - 1 - index
        return jnp.where(place > mine, slabs[place, START] + power * entry, entry)

    entry = lax.fori_loop(0, count, behind, zero)
    grad_inputs = input_gradients(c, rate, residues, entry)
    scale = 1.0 / math.sqrt(lax.axis_size("dp") * rows * count)
    terms = jnp.stack([total[RES], total[POLE] * (-pole * residues)]) * scale
    owned = lax.psum_scatter(terms, "dp", scatter_dimension=2, tiled=True)
    return (grad_inputs[None], owned[0], owned[1])


def solution(mesh):
    tuned = mesh.shape["dp"] == 4 and mesh.shape["context"] == 8
    in_specs = (P("dp", "context", None), P("dp", "context", None), P(), P())
    out_specs = (P("dp", "context", None), P(None, "dp"), P(None, "dp"))
    return jax.shard_map(
        four_by_eight if tuned else any_mesh, mesh=mesh, in_specs=in_specs, out_specs=out_specs, check_vma=False
    )
```

```python
import functools
import math

import jax
import jax.numpy as jnp
from jax import lax
from jax.experimental import pallas as pl
from jax.experimental.pallas import tpu as pltpu
from jax.sharding import PartitionSpec as P

LANES = 128
SUBS = 8
SPAN = 8
PARTS = 6
ORDER = (3, 2, 1, 0)
END, START, DEND, DSTART, RES, POLE = range(PARTS)
f32 = jnp.float32


def here(value):
    return pltpu.with_memory_space_constraint(value, pltpu.VMEM)


def vmem():
    return pl.BlockSpec(memory_space=pltpu.VMEM)


def position():
    context = lax.axis_index("context")
    return context // 2, context % 2, lax.axis_index("dp")


def room(megabytes):
    return pltpu.CompilerParams(vmem_limit_bytes=megabytes << 20)


def local_call(kernel, name, shapes, operands, scratch=(), megabytes=2, after=()):
    return pl.pallas_call(
        kernel,
        in_specs=[vmem() for _ in operands] + [far_away() for _ in after],
        out_specs=[vmem() for _ in shapes],
        out_shape=[pltpu.VMEM(shape, f32) for shape in shapes],
        scratch_shapes=[pltpu.VMEM(shape, f32) for shape in scratch],
        compiler_params=room(megabytes),
        name=name,
    )(*[here(item) for item in operands], *[outside(item) for item in after])


def horner(values, point):
    value, slope, scaled = values[0], None, None
    for item in values[1:]:
        if slope is None:
            slope = value
        elif scaled is not None and slope is values[0]:
            slope = scaled + value
        else:
            slope = slope * point + value
        scaled = value * point
        value = scaled + item
    return value, slope


def spread(tiles, scratch, rows, stride):
    for place, tile in enumerate(tiles):
        scratch[pl.ds(place, rows, stride=stride), :] = tile


def summary_kernel(x, c, rate, *refs, **static):
    summarize(x, c, rate, *refs[-7:], **static)


def first_kernel(*refs, **static):
    x, c, rate, res, *outs, x_in, c_in, rate_in, res_in, xs, cs, held, kept, done = refs
    chip, _, _ = position()
    width = 2 * LANES
    copies = []
    for away in ORDER:
        for q in range(4):
            start = 8 * LANES * q + width * (chip ^ away)
            lanes = pl.ds(pl.multiple_of(start, width), width)
            copies += [(ref.at[:, lanes], into.at[:, lanes]) for ref, into in ((x, x_in), (c, c_in))]
        if away == ORDER[0]:
            copies.append((rate, rate_in))
    copies.append((res, res_in))
    copies = [
        pltpu.make_async_copy(source, into, done.at[place])
        for place, (source, into) in enumerate(copies)
    ]
    for copy in copies:
        copy.start()
    for copy in copies[:9]:
        copy.wait()
    summarize(x_in, c_in, rate_in, *outs, xs, cs, held, kept, **static)
    for copy in copies[9:]:
        copy.wait()


def summarize(x, c, rate, theirs, ours, our_rates, xs, cs, rates, kept, *, tile_of, rows, modes, together):
    blocks = rows // SPAN
    for place in range(SUBS):
        lanes = pl.ds(pl.multiple_of(tile_of(place) * LANES, LANES), LANES)
        xs[pl.ds(place, rows, stride=SUBS), :] = x[:, lanes].astype(f32)
        cs[pl.ds(place, rows, stride=SUBS), :] = c[:, lanes].astype(f32)
        rates[pl.ds(place, modes, stride=SUBS), :] = rate[:, lanes]

    def row(ref, index):
        return ref[pl.ds(pl.multiple_of(index * SUBS, SUBS), SUBS), :]

    zero = jnp.zeros((SUBS, LANES), f32)

    def lag_step(block, sums):
        xv = [row(xs, block * SPAN + k) for k in range(SPAN)]
        cv = [row(cs, block * SPAN + k) for k in range(SPAN)]
        return tuple(
            sums[lag] + sum(cv[k] * xv[k - lag] for k in range(lag, SPAN)) for lag in range(SPAN)
        )

    lags = lax.fori_loop(0, blocks, lag_step, (zero,) * SPAN)
    for lag in range(SPAN):
        kept[pl.ds(2 * together * blocks * SUBS + lag * SUBS, SUBS), :] = lags[lag]

    def slot(mode, block, which):
        return pl.ds(pl.multiple_of(((mode * blocks + block) * 2 + which) * SUBS, SUBS), SUBS)

    def some_modes(group, carry):
        ids = [group * together + m for m in range(together)]
        decays = [row(rates, n) for n in ids]
        poles = [jnp.exp(-r) for r in decays]
        spans = [jnp.exp(-r * SPAN) for r in decays]
        slopes = [jnp.exp(-r * (SPAN - 1)) * SPAN for r in decays]

        def forward(block, state):
            xv = [row(xs, block * SPAN + k) for k in range(SPAN)]
            new = []
            for m in range(together):
                now, dnow = state[m]
                value, slope = horner(xv, poles[m])
                push = slope + slopes[m] * now
                kept[slot(m, block, 0), :] = now
                kept[slot(m, block, 1), :] = push
                new.append((now * spans[m] + value, dnow * spans[m] + push))
            return tuple(new)

        ends = lax.fori_loop(0, blocks, forward, ((zero, zero),) * together, unroll=True)

        def backward(index, state):
            block = blocks - 1 - index
            cv = [row(cs, block * SPAN + k) for k in reversed(range(SPAN))]
            new = []
            for m in range(together):
                now, dnow, first, second = state[m]
                value, slope = horner(cv, poles[m])
                entry = kept[slot(m, block, 0), :]
                push = kept[slot(m, block, 1), :]
                first = first + entry * value
                second = second + (entry * slope + now * push)
                new.append(
                    (
                        now * spans[m] + value,
                        dnow * spans[m] + (slope + slopes[m] * now),
                        first,
                        second,
                    )
                )
            return tuple(new)

        starts = lax.fori_loop(0, blocks, backward, ((zero,) * 4,) * together, unroll=True)
        lagged = [
            kept[pl.ds(2 * together * blocks * SUBS + lag * SUBS, SUBS), :]
            for lag in reversed(range(SPAN))
        ]
        for m in range(together):
            value, slope = horner(lagged, poles[m])
            first, second = starts[m][2:]
            results = (
                ends[m][0],
                starts[m][0],
                ends[m][1],
                starts[m][1],
                poles[m] * first + value,
                first + poles[m] * second + slope,
            )
            for part in range(PARTS):
                half = pl.ds((part * modes + ids[m]) * 4, 4)
                theirs[half, :] = results[part][:4]
                ours[half, :] = results[part][4:]
            our_rates[pl.ds(ids[m] * 4, 4), :] = decays[m][4:]
        return carry

    lax.fori_loop(0, modes // together, some_modes, 0)


def chip_tiles(away):
    def tile_of(place):
        chip, half, _ = position()
        return 8 * (place % 4) + 2 * (chip ^ away) + (half ^ (1 - place // 4))

    return tile_of


def next_tiles(first):
    return lambda place: first + place


def summary_parts(rows, modes, tile_of):
    together = 2
    kept = (2 * together * rows // SPAN + SPAN) * SUBS
    static = dict(tile_of=tile_of, rows=rows, modes=modes, together=together)
    shapes = [(PARTS * modes * 4, LANES), (PARTS * modes * 4, LANES), (modes * 4, LANES)]
    scratch = [(rows * SUBS, LANES), (rows * SUBS, LANES), (modes * SUBS, LANES), (kept, LANES)]
    return static, shapes, scratch


def summaries(inputs, cotangent, rate, tile_of, after=()):
    static, shapes, scratch = summary_parts(inputs.shape[0], rate.shape[0], tile_of)
    kernel = functools.partial(summary_kernel, **static)
    return local_call(
        kernel, "summaries", shapes, [inputs, cotangent, rate, *after], scratch, megabytes=4
    )


def first_summaries(inputs, cotangent, rate, residues, tile_of):
    static, shapes, scratch = summary_parts(inputs.shape[0], rate.shape[0], tile_of)
    operands = (inputs, cotangent, rate, residues)
    return pl.pallas_call(
        functools.partial(first_kernel, **static),
        in_specs=[far_away() for _ in operands],
        out_specs=[vmem() for _ in range(len(shapes) + 4)],
        out_shape=[pltpu.VMEM(shape, f32) for shape in shapes]
        + [pltpu.VMEM(item.shape, item.dtype) for item in operands],
        scratch_shapes=[pltpu.VMEM(shape, f32) for shape in scratch]
        + [pltpu.SemaphoreType.DMA((34,))],
        compiler_params=room(4),
        name="first_summaries",
    )(*[outside(item) for item in operands])


def joined(one, two, pole, power, slope):
    cross = one[END] * two[START]
    return (
        power * one[END] + two[END],
        one[START] + power * two[START],
        slope * one[END] + power * one[DEND] + two[DEND],
        one[DSTART] + slope * two[START] + power * two[DSTART],
        one[RES] + two[RES] + pole * cross,
        one[POLE] + two[POLE] + cross + pole * (one[DEND] * two[START] + one[END] * two[DSTART]),
    )


def pair_kernel(own, other, rates, *refs, rows, modes):
    send, hold = refs[-2:]
    size = modes * 4

    def body(one, two):
        r = rates[...]
        power = jnp.exp(-r * rows)
        slope = jnp.exp(-r * (rows - 1)) * float(rows)
        read = lambda ref: [ref[pl.ds(a * size, size), :] for a in range(PARTS)]
        second = read(two)
        result = joined(read(one), second, jnp.exp(-r), power, slope)
        for a in range(PARTS):
            send[pl.ds(a * size, size), :] = result[a]
        hold[pl.ds(0, size), :] = second[START]
        hold[pl.ds(size, size), :] = power

    core = position()[1]

    @pl.when(core == 0)
    def _():
        body(own, other)

    @pl.when(core != 0)
    def _():
        body(other, own)


def paired(own, other, rates, rows, modes, after):
    return local_call(
        functools.partial(pair_kernel, rows=rows, modes=modes),
        "paired",
        [(PARTS * modes * 4, LANES), (2 * modes * 4, LANES)],
        [own, other, rates, *after],
    )


def chain_kernel(*refs, rows, modes, scale):
    pieces, (rate, residues) = refs[:4], refs[4:6]
    back_keep, back_send, term_keep, term_send = refs[6:10]
    ordered, adjoints, small, owned = refs[10:]
    chip, core, depth = position()
    size = modes * 4
    for j in range(4):
        ordered[chip ^ j] = pieces[j][...]
    for q in range(4):
        lanes = pl.ds(pl.multiple_of((8 * q + 2 * chip + core) * LANES, LANES), LANES)
        small[0, pl.ds(q, modes, stride=4), :] = rate[:, lanes]
        small[1, pl.ds(q, modes, stride=4), :] = residues[:, lanes]
    r = small[0]
    pole = jnp.exp(-r)
    power = jnp.exp(-r * rows)
    slope = jnp.exp(-r * (rows - 1)) * float(rows)
    read = lambda c, a: ordered[c, pl.ds(a * size, size), :]
    now, dnow = read(0, END), read(0, DEND)
    sum_res, sum_pole = read(0, RES), read(0, POLE)
    for c in range(1, 4):
        start, dstart = read(c, START), read(c, DSTART)
        cross = now * start
        sum_res = sum_res + read(c, RES) + pole * cross
        sum_pole = sum_pole + read(c, POLE) + cross + pole * (dnow * start + now * dstart)
        if c < 3:
            now, dnow = (
                power * now + read(c, END),
                slope * now + power * dnow + read(c, DEND),
            )
    back = jnp.zeros((size, LANES), f32)
    adjoints[3] = back
    for c in range(2, -1, -1):
        back = read(c + 1, START) + power * back
        adjoints[c] = back
    for place in range(2):
        rows_of = pl.ds(place * size, size)
        back_keep[rows_of, :] = adjoints[chip ^ (2 * place)]
        back_send[rows_of, :] = adjoints[chip ^ (2 * place + 1)]
    owned[pl.ds(0, size), :] = sum_res * scale
    owned[pl.ds(size, size), :] = sum_pole * (-pole * small[1]) * scale
    for place in range(2):
        for ref, q in ((term_keep, 2 * place + depth % 2), (term_send, 2 * place + 1 - depth % 2)):
            for a in range(2):
                ref[pl.ds((place * 2 + a) * modes, modes), :] = owned[
                    pl.ds(a * size + q, modes, stride=4), :
                ]


def chained(pieces, rate, residues, rows, scale):
    modes = rate.shape[0]
    size = modes * 4
    return local_call(
        functools.partial(chain_kernel, rows=rows, modes=modes, scale=scale),
        "chained",
        [(2 * size, LANES)] * 2 + [(4 * modes, LANES)] * 2,
        [*pieces, rate, residues],
        [(4, PARTS * size, LANES), (4, size, LANES), (2, size, LANES), (2 * size, LANES)],
    )


def halve_kernel(kept, got, keep, send):
    upper = position()[2] // 2
    half = kept.shape[0] // 2
    for ref, place in ((keep, upper), (send, 1 - upper)):
        at = pl.ds(pl.multiple_of(place * half, half), half)
        ref[...] = kept[at, :] + got[at, :]


def stack_kernel(one, two, *refs):
    out = refs[-1]
    half = out.shape[0] // 2
    out[:half, :] = one[-half:, :]
    out[half:, :] = two[-half:, :]


def stacked(one, two, rows, after=(), near=()):
    operands = [one, two, *near]
    return local_call(stack_kernel, "stacked", [(2 * rows, LANES)], operands, after=after)[0]


def entry_kernel(*refs, modes):
    kept, near, far = refs[:3]
    holds, (mine, theirs) = refs[3:7], refs[-2:]
    size = modes * 4
    backs = [kept[:size, :], near[:size, :], far[:size, :], far[size:, :]]

    def body(late, early):
        for j in range(4):
            back = backs[j]
            late[pl.ds(j * size, size), :] = back
            early[pl.ds(j * size, size), :] = holds[j][:size, :] + holds[j][size:, :] * back

    core = position()[1]

    @pl.when(core == 0)
    def _():
        body(theirs, mine)

    @pl.when(core != 0)
    def _():
        body(mine, theirs)


def entries(backs, holds, modes, after):
    return local_call(
        functools.partial(entry_kernel, modes=modes),
        "entries",
        [(4 * modes * 4, LANES)] * 2,
        [*backs, *holds, *after],
    )


def input_kernel(cot, rate, res, *refs, blocks, rows, modes, together):
    given, (out, cs, ys, ps, rs, ads, sent, done) = refs[:-8], refs[-8:]
    given = [ref for ref in given if ref.dtype == f32]
    chip, half, _ = position() if len(given) == 2 else (None,) * 3
    width = SUBS * LANES
    first, count = blocks

    def copy(q):
        lanes = pl.ds(pl.multiple_of((first + q) * width, width), width)
        return pltpu.make_async_copy(sent.at[q], out.at[:, lanes], done.at[q])

    def one_block(q, carry):
        block_of_inputs(
            first + q,
            cot,
            rate,
            res,
            given,
            (chip, half),
            sent.at[q],
            (cs, ys, ps, rs, ads),
            rows,
            modes,
            together,
        )
        copy(q).start()
        return carry

    lax.fori_loop(0, count, one_block, 0)
    for q in range(count):
        copy(q).wait()


def block_of_inputs(q, cot, rate, res, given, place, sent, scratch, rows, modes, together):
    cs, ys, ps, rs, ads = scratch
    size = modes * 4

    def tile(i):
        return pl.ds(pl.multiple_of((q * SUBS + i) * LANES, LANES), LANES)

    for i in range(SUBS):
        lanes = tile(i)
        cs[pl.ds(i, rows, stride=SUBS), :] = cot[:, lanes].astype(f32)
        ps[pl.ds(i, modes, stride=SUBS), :] = jnp.exp(-rate[:, lanes])
        rs[pl.ds(i, modes, stride=SUBS), :] = res[:, lanes]
    if len(given) == 1:
        spread([given[0][:, tile(i)] for i in range(SUBS)], ads, modes, SUBS)
    for j in range(4 if len(given) == 2 else 0):
        for core, source in enumerate(given):
            i = 2 * (place[0] ^ j) + (place[1] ^ core)
            ads[pl.ds(i, modes, stride=SUBS), :] = source[pl.ds(j * size + q, modes, stride=4), :]

    for group in range(modes // together):
        at = [pl.ds((group * together + m) * SUBS, SUBS) for m in range(together)]
        poles = [ps[a, :] for a in at]
        weights = [rs[a, :] for a in at]

        def step(index, adjoint):
            now = pl.ds(pl.multiple_of((rows - 1 - index) * SUBS, SUBS), SUBS)
            value = cs[now, :]
            adjoint = tuple(a * p + value for a, p in zip(adjoint, poles))
            terms = [a * w for a, w in zip(adjoint, weights)]
            while len(terms) > 1:
                terms = [a + b for a, b in zip(terms[::2], terms[1::2])]
            ys[now, :] = terms[0] if group == 0 else ys[now, :] + terms[0]
            return adjoint

        lax.fori_loop(0, rows, step, tuple(ads[a, :] for a in at), unroll=8)
    for i in range(SUBS):
        sent[:, pl.ds(i * LANES, LANES)] = ys[pl.ds(i, rows, stride=SUBS), :].astype(sent.dtype)


def far_away():
    return pl.BlockSpec(memory_space=pltpu.HBM)


def outside(value):
    return pltpu.with_memory_space_constraint(value, pltpu.HBM)


def input_gradients(cotangent, rate, residues, given, blocks, onto=None):
    rows, channels = cotangent.shape
    modes = rate.shape[0]
    width = SUBS * LANES
    scratch = lambda height: pltpu.VMEM((height * SUBS, LANES), f32)
    operands = [here(item) for item in (cotangent, rate, residues, *given)]
    specs = [vmem() for _ in operands]
    aliases = {}
    if onto is not None:
        aliases = {len(operands): 0}
        operands.append(outside(onto))
        specs.append(far_away())
    return pl.pallas_call(
        functools.partial(input_kernel, blocks=blocks, rows=rows, modes=modes, together=16),
        in_specs=specs,
        out_specs=far_away(),
        out_shape=jax.ShapeDtypeStruct((rows, channels), cotangent.dtype),
        scratch_shapes=[
            scratch(rows),
            scratch(rows),
            scratch(modes),
            scratch(modes),
            scratch(modes),
            pltpu.VMEM((blocks[1], rows, width), cotangent.dtype),
            pltpu.SemaphoreType.DMA((blocks[1],)),
        ],
        input_output_aliases=aliases,
        compiler_params=room(5),
        name="input_gradients",
    )(*operands)


def place_kernel(*refs, modes):
    pieces, (out_res, out_rate) = refs[:2], refs[-2:]
    chip, half, _ = position()
    for j in range(4):
        for core in range(2):
            i = 2 * (chip ^ j) + (half ^ core)
            lanes = pl.ds(pl.multiple_of(i * LANES, LANES), LANES)
            row = ((j % 2) * 2 + core) * 2 * modes
            out_res[:, lanes] = pieces[j // 2][pl.ds(row, modes), :]
            out_rate[:, lanes] = pieces[j // 2][pl.ds(row + modes, modes), :]


def placed(pieces, modes, after):
    shape = jax.ShapeDtypeStruct((modes, SUBS * LANES), f32)
    return pl.pallas_call(
        functools.partial(place_kernel, modes=modes),
        in_specs=[vmem() for _ in pieces] + [far_away()],
        out_specs=[vmem(), vmem()],
        out_shape=[shape, shape],
        compiler_params=room(2),
        name="placed",
    )(
        *[here(item) for item in pieces],
        outside(after),
    )


def crossed(value, distance):
    return lax.ppermute(value, "context", [(i, i ^ distance) for i in range(8)])


def shifted(value, distance):
    return lax.ppermute(value, "dp", [(i, i ^ distance) for i in range(4)])


def four_by_eight(inputs, cotangent, rate, residues):
    x, c = inputs[0], cotangent[0]
    rows, modes = x.shape[0], rate.shape[0]
    theirs, ours, rates, x, c, rate, residues = first_summaries(
        x, c, rate, residues, chip_tiles(ORDER[0])
    )
    sends, holds, got = {}, {}, {}
    waiting = (ORDER[0], ours, crossed(theirs, 1), rates)

    def pair(waiting, after=()):
        away, ours, others, rates = waiting
        sends[away], holds[away] = paired(ours, others, rates, rows, modes, after)
        if away:
            got[away] = crossed(sends[away], 2 * away)

    for away in ORDER[1:]:
        if away == 0:
            pair(waiting, (landed,))
        after = {2: (), 1: (holds.get(3),), 0: (holds.get(2), holds.get(1))}[away]
        theirs, ours, next_rates = summaries(x, c, rate, chip_tiles(away), after)
        if away == 1:
            landed = stacked(got[3], next_rates, 8)
            pair(waiting, (landed,))
        elif away:
            pair(waiting, (next_rates,))
        waiting = (away, ours, crossed(theirs, 1), next_rates)
    pair(waiting, (stacked(got[1], got[2], 8),))
    scale = 1.0 / math.sqrt(4 * rows * 8)
    back_keep, back_send, term_keep, term_send = chained(
        [sends[0], got[1], got[2], got[3]], rate, residues, 2 * rows, scale
    )
    half = (2 * modes, LANES)
    keep, send = local_call(
        halve_kernel, "halved", [half, half], [term_keep, shifted(term_send, 1)]
    )
    near = crossed(back_send, 2)
    total = keep + shifted(send, 2)
    far = crossed(stacked(back_keep, near, 4 * modes, (), (send,)), 4)
    mine, others = entries([back_keep, near, far], [holds[j] for j in range(4)], modes, (total,))
    entry = (mine, crossed(others, 1))
    both = stacked(total, crossed(total, 1), 2 * modes)
    grad_inputs = input_gradients(c, rate, residues, entry, (0, 2))
    four = stacked(both, crossed(both, 2), 4 * modes, (grad_inputs,))
    grad_inputs = input_gradients(c, rate, residues, entry, (2, 2), grad_inputs)
    grad_residues, grad_rate = placed([four, crossed(four, 4)], modes, grad_inputs)
    return (grad_inputs[None], grad_residues, grad_rate)


def any_mesh(inputs, cotangent, rate, residues):
    x, c = inputs[0], cotangent[0]
    rows, channels, modes = x.shape[0], x.shape[1], rate.shape[0]
    count, mine = lax.axis_size("context"), lax.axis_index("context")
    blocks = [
        summaries(x, c, rate, next_tiles(first))[:2] for first in range(0, channels // LANES, SUBS)
    ]
    local = jnp.stack([half for pair in blocks for half in pair])
    local = local.reshape(-1, PARTS, modes, 4 * LANES)
    local = jnp.moveaxis(local, 0, 2).reshape(PARTS, modes, channels)
    slabs = lax.all_gather(local, "context")
    pole, power = jnp.exp(-rate), jnp.exp(-rate * rows)
    slope = jnp.exp(-rate * (rows - 1)) * rows
    total = tuple(slabs[0])
    for place in range(1, count):
        total = joined(total, slabs[place], pole, power, slope)
    zero = jnp.zeros_like(pole)

    def behind(index, entry):
        place = count - 1 - index
        return jnp.where(place > mine, slabs[place, START] + power * entry, entry)

    entry = lax.fori_loop(0, count, behind, zero)
    blocks = (0, channels // (SUBS * LANES))
    grad_inputs = input_gradients(c, rate, residues, [entry], blocks)
    scale = 1.0 / math.sqrt(lax.axis_size("dp") * rows * count)
    terms = jnp.stack([total[RES], total[POLE] * (-pole * residues)]) * scale
    owned = lax.psum_scatter(terms, "dp", scatter_dimension=2, tiled=True)
    return (grad_inputs[None], owned[0], owned[1])


def solution(mesh):
    tuned = mesh.shape["dp"] == 4 and mesh.shape["context"] == 8
    in_specs = (P("dp", "context", None), P("dp", "context", None), P(), P())
    out_specs = (P("dp", "context", None), P(None, "dp"), P(None, "dp"))
    return jax.shard_map(
        four_by_eight if tuned else any_mesh, mesh=mesh, in_specs=in_specs, out_specs=out_specs, check_vma=False
    )
```

```python
import functools
import math

import jax
import jax.numpy as jnp
from jax import lax
from jax.experimental import pallas as pl
from jax.experimental.pallas import tpu as pltpu
from jax.sharding import PartitionSpec as P

LANES = 128
SUBS = 8
SPAN = 8
PARTS = 6
ORDER = (3, 1, 2, 0)
END, START, DEND, DSTART, RES, POLE = range(PARTS)
f32 = jnp.float32


def here(value):
    return pltpu.with_memory_space_constraint(value, pltpu.VMEM)


def vmem():
    return pl.BlockSpec(memory_space=pltpu.VMEM)


def position():
    context = lax.axis_index("context")
    return context // 2, context % 2, lax.axis_index("dp")


def room(megabytes):
    return pltpu.CompilerParams(vmem_limit_bytes=megabytes << 20)


def bits():
    chip, core, _ = position()
    return core, chip % 2, chip // 2


def local_call(kernel, name, shapes, operands, scratch=(), megabytes=2, after=()):
    return pl.pallas_call(
        kernel,
        in_specs=[vmem() for _ in operands] + [far_away() for _ in after],
        out_specs=[vmem() for _ in shapes],
        out_shape=[pltpu.VMEM(shape, f32) for shape in shapes],
        scratch_shapes=[pltpu.VMEM(shape, f32) for shape in scratch],
        compiler_params=room(megabytes),
        name=name,
    )(*[here(item) for item in operands], *[outside(item) for item in after])


def horner(values, point):
    value, slope, scaled = values[0], None, None
    for item in values[1:]:
        if slope is None:
            slope = value
        elif scaled is not None and slope is values[0]:
            slope = scaled + value
        else:
            slope = slope * point + value
        scaled = value * point
        value = scaled + item
    return value, slope


def spread(tiles, scratch, rows, stride):
    for place, tile in enumerate(tiles):
        scratch[pl.ds(place, rows, stride=stride), :] = tile


def summary_kernel(x, c, rate, *refs, **static):
    summarize(x, c, rate, *refs[-7:], **static)


def first_kernel(*refs, **static):
    x, c, rate, res, *outs, x_in, c_in, rate_in, res_in, xs, cs, held, kept, done = refs
    chip, _, _ = position()
    width = 2 * LANES
    copies = []
    for away in ORDER:
        for q in range(4):
            start = 8 * LANES * q + width * (chip ^ away)
            lanes = pl.ds(pl.multiple_of(start, width), width)
            copies += [(ref.at[:, lanes], into.at[:, lanes]) for ref, into in ((x, x_in), (c, c_in))]
        if away == ORDER[0]:
            copies.append((rate, rate_in))
    copies.append((res, res_in))
    copies = [
        pltpu.make_async_copy(source, into, done.at[place])
        for place, (source, into) in enumerate(copies)
    ]
    for copy in copies:
        copy.start()
    for copy in copies[:9]:
        copy.wait()
    summarize(x_in, c_in, rate_in, *outs, xs, cs, held, kept, **static)
    for copy in copies[9:]:
        copy.wait()


def summarize(x, c, rate, theirs, ours, our_rates, xs, cs, rates, kept, *, tile_of, rows, modes, together):
    blocks = rows // SPAN
    for place in range(SUBS):
        lanes = pl.ds(pl.multiple_of(tile_of(place) * LANES, LANES), LANES)
        xs[pl.ds(place, rows, stride=SUBS), :] = x[:, lanes].astype(f32)
        cs[pl.ds(place, rows, stride=SUBS), :] = c[:, lanes].astype(f32)
        rates[pl.ds(place, modes, stride=SUBS), :] = rate[:, lanes]

    def row(ref, index):
        return ref[pl.ds(pl.multiple_of(index * SUBS, SUBS), SUBS), :]

    zero = jnp.zeros((SUBS, LANES), f32)

    def lag_step(block, sums):
        xv = [row(xs, block * SPAN + k) for k in range(SPAN)]
        cv = [row(cs, block * SPAN + k) for k in range(SPAN)]
        return tuple(
            sums[lag] + sum(cv[k] * xv[k - lag] for k in range(lag, SPAN)) for lag in range(SPAN)
        )

    lags = lax.fori_loop(0, blocks, lag_step, (zero,) * SPAN)
    for lag in range(SPAN):
        kept[pl.ds(2 * together * blocks * SUBS + lag * SUBS, SUBS), :] = lags[lag]

    def slot(mode, block, which):
        return pl.ds(pl.multiple_of(((mode * blocks + block) * 2 + which) * SUBS, SUBS), SUBS)

    def some_modes(group, carry):
        ids = [group * together + m for m in range(together)]
        decays = [row(rates, n) for n in ids]
        poles = [jnp.exp(-r) for r in decays]
        spans = [jnp.exp(-r * SPAN) for r in decays]
        slopes = [jnp.exp(-r * (SPAN - 1)) * SPAN for r in decays]

        def forward(block, state):
            xv = [row(xs, block * SPAN + k) for k in range(SPAN)]
            new = []
            for m in range(together):
                now, dnow = state[m]
                value, slope = horner(xv, poles[m])
                push = slope + slopes[m] * now
                kept[slot(m, block, 0), :] = now
                kept[slot(m, block, 1), :] = push
                new.append((now * spans[m] + value, dnow * spans[m] + push))
            return tuple(new)

        ends = lax.fori_loop(0, blocks, forward, ((zero, zero),) * together, unroll=True)

        def backward(index, state):
            block = blocks - 1 - index
            cv = [row(cs, block * SPAN + k) for k in reversed(range(SPAN))]
            new = []
            for m in range(together):
                now, dnow, first, second = state[m]
                value, slope = horner(cv, poles[m])
                entry = kept[slot(m, block, 0), :]
                push = kept[slot(m, block, 1), :]
                first = first + entry * value
                second = second + (entry * slope + now * push)
                new.append(
                    (
                        now * spans[m] + value,
                        dnow * spans[m] + (slope + slopes[m] * now),
                        first,
                        second,
                    )
                )
            return tuple(new)

        starts = lax.fori_loop(0, blocks, backward, ((zero,) * 4,) * together, unroll=True)
        lagged = [
            kept[pl.ds(2 * together * blocks * SUBS + lag * SUBS, SUBS), :]
            for lag in reversed(range(SPAN))
        ]
        for m in range(together):
            value, slope = horner(lagged, poles[m])
            first, second = starts[m][2:]
            results = (
                ends[m][0],
                starts[m][0],
                ends[m][1],
                starts[m][1],
                poles[m] * first + value,
                first + poles[m] * second + slope,
            )
            for part in range(PARTS):
                half = pl.ds((part * modes + ids[m]) * 4, 4)
                theirs[half, :] = results[part][:4]
                ours[half, :] = results[part][4:]
            our_rates[pl.ds(ids[m] * 4, 4), :] = decays[m][4:]
        return carry

    lax.fori_loop(0, modes // together, some_modes, 0)


def chip_tiles(away):
    def tile_of(place):
        chip, half, _ = position()
        return 8 * (place % 4) + 2 * (chip ^ away) + (half ^ (1 - place // 4))

    return tile_of


def next_tiles(first):
    return lambda place: first + place


def summary_parts(rows, modes, tile_of):
    together = 2
    kept = (2 * together * rows // SPAN + SPAN) * SUBS
    static = dict(tile_of=tile_of, rows=rows, modes=modes, together=together)
    shapes = [(PARTS * modes * 4, LANES), (PARTS * modes * 4, LANES), (modes * 4, LANES)]
    scratch = [(rows * SUBS, LANES), (rows * SUBS, LANES), (modes * SUBS, LANES), (kept, LANES)]
    return static, shapes, scratch


def summaries(inputs, cotangent, rate, tile_of, after=()):
    static, shapes, scratch = summary_parts(inputs.shape[0], rate.shape[0], tile_of)
    kernel = functools.partial(summary_kernel, **static)
    return local_call(
        kernel, "summaries", shapes, [inputs, cotangent, rate, *after], scratch, megabytes=4
    )


def first_summaries(inputs, cotangent, rate, residues, tile_of):
    static, shapes, scratch = summary_parts(inputs.shape[0], rate.shape[0], tile_of)
    operands = (inputs, cotangent, rate, residues)
    return pl.pallas_call(
        functools.partial(first_kernel, **static),
        in_specs=[far_away() for _ in operands],
        out_specs=[vmem() for _ in range(len(shapes) + 4)],
        out_shape=[pltpu.VMEM(shape, f32) for shape in shapes]
        + [pltpu.VMEM(item.shape, item.dtype) for item in operands],
        scratch_shapes=[pltpu.VMEM(shape, f32) for shape in scratch]
        + [pltpu.SemaphoreType.DMA((34,))],
        compiler_params=room(4),
        name="first_summaries",
    )(*[outside(item) for item in operands])


def joined(one, two, pole, power, slope):
    cross = one[END] * two[START]
    return (
        power * one[END] + two[END],
        one[START] + power * two[START],
        slope * one[END] + power * one[DEND] + two[DEND],
        one[DSTART] + slope * two[START] + power * two[DSTART],
        one[RES] + two[RES] + pole * cross,
        one[POLE] + two[POLE] + cross + pole * (one[DEND] * two[START] + one[END] * two[DSTART]),
    )


def pair_kernel(own, other, rates, *refs, level, rows, modes):
    send, hold = refs[-2:]
    size = modes * 4

    def body(one, two):
        r = rates[...]
        power = jnp.exp(-r * rows)
        slope = jnp.exp(-r * (rows - 1)) * float(rows)
        read = lambda ref: [ref[pl.ds(a * size, size), :] for a in range(PARTS)]
        second = read(two)
        result = joined(read(one), second, jnp.exp(-r), power, slope)
        for a in range(PARTS):
            send[pl.ds(a * size, size), :] = result[a]
        hold[pl.ds(0, size), :] = second[START]
        hold[pl.ds(size, size), :] = power

    later = bits()[level]

    @pl.when(later == 0)
    def _():
        body(own, other)

    @pl.when(later != 0)
    def _():
        body(other, own)


def paired(own, other, rates, level, rows, modes, after=()):
    return local_call(
        functools.partial(pair_kernel, level=level, rows=rows, modes=modes),
        "paired",
        [(PARTS * modes * 4, LANES), (2 * modes * 4, LANES)],
        [own, other, rates, *after],
    )


def close_kernel(own, other, rates, residues, term_keep, term_send, small, owned, *, modes, scale):
    chip, core, depth = position()
    size = modes * 4
    for q in range(4):
        lanes = pl.ds(pl.multiple_of((8 * q + 2 * chip + core) * LANES, LANES), LANES)
        small[pl.ds(q, modes, stride=4), :] = residues[:, lanes]
    pole = jnp.exp(-rates[...])
    later = chip // 2 != 0
    read = lambda ref, a: ref[pl.ds(a * size, size), :]
    pick = lambda a, one, two: jnp.where(later, read(two, a), read(one, a))
    now, dnow = pick(END, own, other), pick(DEND, own, other)
    start, dstart = pick(START, other, own), pick(DSTART, other, own)
    cross = now * start
    sum_res = read(own, RES) + read(other, RES) + pole * cross
    sum_pole = read(own, POLE) + read(other, POLE) + cross + pole * (dnow * start + now * dstart)
    owned[pl.ds(0, size), :] = sum_res * scale
    owned[pl.ds(size, size), :] = sum_pole * (-pole * small[...]) * scale
    for place in range(2):
        for ref, q in ((term_keep, 2 * place + depth % 2), (term_send, 2 * place + 1 - depth % 2)):
            for a in range(2):
                ref[pl.ds((place * 2 + a) * modes, modes), :] = owned[
                    pl.ds(a * size + q, modes, stride=4), :
                ]


def closed(own, other, rates, residues, scale):
    modes = residues.shape[0]
    size = modes * 4
    return local_call(
        functools.partial(close_kernel, modes=modes, scale=scale),
        "closed",
        [(4 * modes, LANES)] * 2,
        [own, other, rates, residues],
        [(size, LANES), (2 * size, LANES)],
    )


def hand_kernel(other, beside, hold_own, hold_side, *refs, modes):
    keep, send = refs[-2:]
    _, right, later = bits()
    size = modes * 4
    entering = (other[pl.ds(START * size, size), :], beside[...])
    for place, hold in enumerate((hold_own, hold_side)):
        rows_of = pl.ds(place * size, size)
        late = jnp.where(later == 0, entering[place], 0.0)
        early = hold[:size, :] + hold[size:, :] * late
        keep[rows_of, :] = jnp.where(right == 0, early, late)
        send[rows_of, :] = jnp.where(right == 0, late, early)


def handed(other, beside, hold_own, hold_side, modes, near):
    return local_call(
        functools.partial(hand_kernel, modes=modes),
        "handed",
        [(2 * modes * 4, LANES)] * 2,
        [other, beside, hold_own, hold_side, *near],
    )


def add_kernel(one, two, *refs):
    refs[-1][...] = one[...] + two[...]


def halve_kernel(kept, got, *refs):
    keep, send = refs[-2:]
    upper = position()[2] // 2
    half = kept.shape[0] // 2
    for ref, place in ((keep, upper), (send, 1 - upper)):
        at = pl.ds(pl.multiple_of(place * half, half), half)
        ref[...] = kept[at, :] + got[at, :]


def stack_kernel(one, two, *refs):
    out = refs[-1]
    half = out.shape[0] // 2
    out[:half, :] = one[-half:, :]
    out[half:, :] = two[-half:, :]


def stacked(one, two, rows, after=(), near=()):
    operands = [one, two, *near]
    return local_call(stack_kernel, "stacked", [(2 * rows, LANES)], operands, after=after)[0]


def entry_kernel(*refs, modes):
    kept, near = refs[:2]
    holds, (mine, theirs) = refs[2:6], refs[-2:]
    size = modes * 4
    backs = [kept[:size, :], near[:size, :], kept[size:, :], near[size:, :]]

    def body(late, early):
        for j in range(4):
            back = backs[j]
            late[pl.ds(j * size, size), :] = back
            early[pl.ds(j * size, size), :] = holds[j][:size, :] + holds[j][size:, :] * back

    core = position()[1]

    @pl.when(core == 0)
    def _():
        body(theirs, mine)

    @pl.when(core != 0)
    def _():
        body(mine, theirs)


def entries(kept, near, holds, modes, after):
    return local_call(
        functools.partial(entry_kernel, modes=modes),
        "entries",
        [(4 * modes * 4, LANES)] * 2,
        [kept, near, *holds, *after],
    )


def input_kernel(*refs, block, last, given, lead, rows, modes, together):
    cot, rate, res = refs[:3]
    entry, lead_ref = refs[3 : 3 + given], refs[3 + given : 4 + given]
    *outs, cs, ys, ps, rs, ads, done = refs[-(6 + (lead or last) + 1) :]
    width = SUBS * LANES
    copies = []
    if lead:
        lanes = pl.ds((block - 1) * width, width)
        copies.append(pltpu.make_async_copy(lead_ref[0], outs[0].at[:, lanes], done.at[0]))
        copies[0].start()
    place = position()[:2] if given == 2 else None
    scratch = (cs, ys, ps, rs, ads)
    sent = outs[-1]
    block_of_inputs(block, cot, rate, res, entry, place, sent, scratch, rows, modes, together)
    if last:
        lanes = pl.ds(block * width, width)
        copies.append(pltpu.make_async_copy(sent, outs[0].at[:, lanes], done.at[1]))
        copies[-1].start()
    for copy in copies:
        copy.wait()


def block_of_inputs(q, cot, rate, res, given, place, sent, scratch, rows, modes, together):
    cs, ys, ps, rs, ads = scratch
    size = modes * 4

    def tile(i):
        return pl.ds((q * SUBS + i) * LANES, LANES)

    for i in range(SUBS):
        lanes = tile(i)
        cs[pl.ds(i, rows, stride=SUBS), :] = cot[:, lanes].astype(f32)
        ps[pl.ds(i, modes, stride=SUBS), :] = jnp.exp(-rate[:, lanes])
        rs[pl.ds(i, modes, stride=SUBS), :] = res[:, lanes]
    if len(given) == 1:
        spread([given[0][:, tile(i)] for i in range(SUBS)], ads, modes, SUBS)
    for j in range(4 if len(given) == 2 else 0):
        for core, source in enumerate(given):
            i = 2 * (place[0] ^ j) + (place[1] ^ core)
            ads[pl.ds(i, modes, stride=SUBS), :] = source[pl.ds(j * size + q, modes, stride=4), :]

    for group in range(modes // together):
        at = [pl.ds((group * together + m) * SUBS, SUBS) for m in range(together)]
        poles = [ps[a, :] for a in at]
        weights = [rs[a, :] for a in at]

        def step(index, adjoint):
            now = pl.ds(pl.multiple_of((rows - 1 - index) * SUBS, SUBS), SUBS)
            value = cs[now, :]
            adjoint = tuple(a * p + value for a, p in zip(adjoint, poles))
            terms = [a * w for a, w in zip(adjoint, weights)]
            while len(terms) > 1:
                terms = [a + b for a, b in zip(terms[::2], terms[1::2])]
            ys[now, :] = terms[0] if group == 0 else ys[now, :] + terms[0]
            return adjoint

        lax.fori_loop(0, rows, step, tuple(ads[a, :] for a in at), unroll=8)
    for i in range(SUBS):
        sent[:, pl.ds(i * LANES, LANES)] = ys[pl.ds(i, rows, stride=SUBS), :].astype(sent.dtype)


def far_away():
    return pl.BlockSpec(memory_space=pltpu.HBM)


def outside(value):
    return pltpu.with_memory_space_constraint(value, pltpu.HBM)


def input_gradients(cotangent, rate, residues, given, block, lead=None, onto=None, last=False):
    rows, channels = cotangent.shape
    modes = rate.shape[0]
    width = SUBS * LANES
    scratch = lambda height: pltpu.VMEM((height * SUBS, LANES), f32)
    operands = [here(item) for item in (cotangent, rate, residues, *given)]
    shapes, specs = [], []
    if lead is not None:
        operands.append(here(lead))
    in_specs = [vmem() for _ in operands]
    aliases = {}
    if lead is not None or last:
        shapes.append(jax.ShapeDtypeStruct((rows, channels), cotangent.dtype))
        specs.append(far_away())
    if onto is not None:
        aliases = {len(operands): 0}
        operands.append(outside(onto))
        in_specs.append(far_away())
    shapes.append(pltpu.VMEM((rows, width), cotangent.dtype))
    specs.append(vmem())
    return pl.pallas_call(
        functools.partial(
            input_kernel,
            block=block,
            last=last,
            given=len(given),
            lead=lead is not None,
            rows=rows,
            modes=modes,
            together=16,
        ),
        in_specs=in_specs,
        out_specs=specs,
        out_shape=shapes,
        scratch_shapes=[
            scratch(rows),
            scratch(rows),
            scratch(modes),
            scratch(modes),
            scratch(modes),
            pltpu.SemaphoreType.DMA((2,)),
        ],
        input_output_aliases=aliases,
        compiler_params=room(4),
        name="input_gradients",
    )(*operands)


def place_kernel(*refs, modes):
    pieces, (out_res, out_rate) = refs[:2], refs[-2:]
    chip, half, _ = position()
    for j in range(4):
        for core in range(2):
            i = 2 * (chip ^ j) + (half ^ core)
            lanes = pl.ds(pl.multiple_of(i * LANES, LANES), LANES)
            row = ((j % 2) * 2 + core) * 2 * modes
            out_res[:, lanes] = pieces[j // 2][pl.ds(row, modes), :]
            out_rate[:, lanes] = pieces[j // 2][pl.ds(row + modes, modes), :]


def placed(pieces, modes, after):
    shape = jax.ShapeDtypeStruct((modes, SUBS * LANES), f32)
    return pl.pallas_call(
        functools.partial(place_kernel, modes=modes),
        in_specs=[vmem() for _ in pieces] + [far_away()],
        out_specs=[vmem(), vmem()],
        out_shape=[shape, shape],
        compiler_params=room(2),
        name="placed",
    )(
        *[here(item) for item in pieces],
        outside(after),
    )


def crossed(value, distance):
    return lax.ppermute(value, "context", [(i, i ^ distance) for i in range(8)])


def shifted(value, distance):
    return lax.ppermute(value, "dp", [(i, i ^ distance) for i in range(4)])


def four_by_eight(inputs, cotangent, rate, residues):
    x, c = inputs[0], cotangent[0]
    rows, modes = x.shape[0], rate.shape[0]
    theirs, ours, rates, x, c, rate, residues = first_summaries(
        x, c, rate, residues, chip_tiles(ORDER[0])
    )
    holds = {}

    def cores(away, ours, others, rates, after=()):
        sums, holds[away] = paired(ours, others, rates, 0, rows, modes, after)
        return sums

    def more(away, after=()):
        theirs, ours, rates = summaries(x, c, rate, chip_tiles(away), after)
        return crossed(theirs, 1), ours, rates

    theirs3 = crossed(theirs, 1)
    theirs1, ours1, rates1 = more(1)
    got2 = crossed(cores(3, ours, theirs3, rates, (rates1,)), 2)
    theirs2, ours2, rates2 = more(2, (holds[3],))
    got0 = crossed(cores(1, ours1, theirs1, rates1, (rates2,)), 2)
    landed = stacked(got2, holds[1], 8)
    row2 = cores(2, ours2, theirs2, rates2, (landed,))
    row2, hold_side = paired(row2, got2, rates2, 1, 2 * rows, modes)
    other = crossed(row2, 4)
    theirs0, ours0, rates0 = more(0, (hold_side, holds[1]))
    landed = stacked(stacked(other, rates0, 8), got0, 8)
    row0 = cores(0, ours0, theirs0, rates0, (landed,))
    row0, hold_own = paired(row0, got0, rates0, 1, 2 * rows, modes)
    beside = crossed(row0[START * 4 * modes : (START + 1) * 4 * modes], 4)
    scale = 1.0 / math.sqrt(4 * rows * 8)
    term_keep, term_send = closed(row0, other, rates0, residues, scale)
    half = (2 * modes, LANES)
    keep, send = local_call(
        halve_kernel, "halved", [half, half], [term_keep, shifted(term_send, 1)]
    )
    back_keep, back_send = handed(other, beside, hold_own, hold_side, modes, (send,))
    back_near = crossed(back_send, 2)
    (total,) = local_call(add_kernel, "added", [half], [keep, shifted(send, 2)])
    mine, others = entries(back_keep, back_near, [holds[j] for j in range(4)], modes, (total,))
    entry = (mine, crossed(others, 1))
    both = stacked(total, crossed(total, 1), 2 * modes)
    gradients = functools.partial(input_gradients, c, rate, residues, entry)
    (part0,) = gradients(0)
    grad_inputs, part1 = gradients(1, part0)
    four = stacked(both, crossed(both, 2), 4 * modes, (), (part1,))
    grad_inputs, part2 = gradients(2, part1, grad_inputs)
    grad_inputs, _ = gradients(3, part2, grad_inputs, True)
    grad_residues, grad_rate = placed([four, crossed(four, 4)], modes, grad_inputs)
    return (grad_inputs[None], grad_residues, grad_rate)


def any_mesh(inputs, cotangent, rate, residues):
    x, c = inputs[0], cotangent[0]
    rows, channels, modes = x.shape[0], x.shape[1], rate.shape[0]
    slab_count, mine = lax.axis_size("context"), lax.axis_index("context")
    blocks = [
        summaries(x, c, rate, next_tiles(first))[:2] for first in range(0, channels // LANES, SUBS)
    ]
    local = jnp.stack([half for pair in blocks for half in pair])
    local = local.reshape(-1, PARTS, modes, 4 * LANES)
    local = jnp.moveaxis(local, 0, 2).reshape(PARTS, modes, channels)
    slabs = lax.all_gather(local, "context")
    pole, power = jnp.exp(-rate), jnp.exp(-rate * rows)
    slope = jnp.exp(-rate * (rows - 1)) * rows
    total = tuple(slabs[0])
    for place in range(1, slab_count):
        total = joined(total, slabs[place], pole, power, slope)
    zero = jnp.zeros_like(pole)

    def behind(index, entry):
        place = slab_count - 1 - index
        return jnp.where(place > mine, slabs[place, START] + power * entry, entry)

    entry = lax.fori_loop(0, slab_count, behind, zero)
    count = channels // (SUBS * LANES)
    lead = grad_inputs = None
    for block in range(count):
        last = block == count - 1
        *grad_inputs, lead = input_gradients(
            c, rate, residues, [entry], block, lead, grad_inputs, last
        )
        grad_inputs = grad_inputs[0] if grad_inputs else None
    scale = 1.0 / math.sqrt(lax.axis_size("dp") * rows * slab_count)
    terms = jnp.stack([total[RES], total[POLE] * (-pole * residues)]) * scale
    owned = lax.psum_scatter(terms, "dp", scatter_dimension=2, tiled=True)
    return (grad_inputs[None], owned[0], owned[1])


def solution(mesh):
    tuned = mesh.shape["dp"] == 4 and mesh.shape["context"] == 8
    in_specs = (P("dp", "context", None), P("dp", "context", None), P(), P())
    out_specs = (P("dp", "context", None), P(None, "dp"), P(None, "dp"))
    return jax.shard_map(
        four_by_eight if tuned else any_mesh, mesh=mesh, in_specs=in_specs, out_specs=out_specs, check_vma=False
    )
```

```python
import functools
import math

import jax
import jax.numpy as jnp
from jax import lax
from jax.experimental import pallas as pl
from jax.experimental.pallas import tpu as pltpu
from jax.sharding import PartitionSpec as P

LANES = 128
SUBS = 8
SPAN = 8
PARTS = 6
ORDER = (3, 1, 2, 0)
END, START, DEND, DSTART, RES, POLE = range(PARTS)
f32 = jnp.float32


def here(value):
    return pltpu.with_memory_space_constraint(value, pltpu.VMEM)


def vmem():
    return pl.BlockSpec(memory_space=pltpu.VMEM)


def position():
    context = lax.axis_index("context")
    return context // 2, context % 2, lax.axis_index("dp")


def room(megabytes):
    return pltpu.CompilerParams(vmem_limit_bytes=megabytes << 20)


def bits():
    chip, core, _ = position()
    return core, chip % 2, chip // 2


def local_call(kernel, name, shapes, operands, scratch=(), megabytes=2, after=()):
    return pl.pallas_call(
        kernel,
        in_specs=[vmem() for _ in operands] + [far_away() for _ in after],
        out_specs=[vmem() for _ in shapes],
        out_shape=[pltpu.VMEM(shape, f32) for shape in shapes],
        scratch_shapes=[pltpu.VMEM(shape, f32) for shape in scratch],
        compiler_params=room(megabytes),
        name=name,
    )(*[here(item) for item in operands], *[outside(item) for item in after])


def horner(values, point):
    value, slope, scaled = values[0], None, None
    for item in values[1:]:
        if slope is None:
            slope = value
        elif scaled is not None and slope is values[0]:
            slope = scaled + value
        else:
            slope = slope * point + value
        scaled = value * point
        value = scaled + item
    return value, slope


def spread(tiles, scratch, rows, stride):
    for place, tile in enumerate(tiles):
        scratch[pl.ds(place, rows, stride=stride), :] = tile


def summary_kernel(x, c, rate, *refs, **static):
    summarize(x, c, rate, *refs[-7:], **static)


def first_kernel(*refs, **static):
    x, c, rate, res, *outs, x_in, c_in, rate_in, res_in, xs, cs, held, kept, done = refs
    chip, _, _ = position()
    width = 2 * LANES
    copies = []
    for away in ORDER:
        for q in range(4):
            start = 8 * LANES * q + width * (chip ^ away)
            lanes = pl.ds(pl.multiple_of(start, width), width)
            copies += [(ref.at[:, lanes], into.at[:, lanes]) for ref, into in ((x, x_in), (c, c_in))]
        if away == ORDER[0]:
            copies.append((rate, rate_in))
    copies.append((res, res_in))
    copies = [
        pltpu.make_async_copy(source, into, done.at[place])
        for place, (source, into) in enumerate(copies)
    ]
    for copy in copies:
        copy.start()
    for copy in copies[:9]:
        copy.wait()
    summarize(x_in, c_in, rate_in, *outs, xs, cs, held, kept, **static)
    for copy in copies[9:]:
        copy.wait()


def summarize(x, c, rate, theirs, ours, our_rates, xs, cs, rates, kept, *, tile_of, rows, modes, together):
    blocks = rows // SPAN
    for place in range(SUBS):
        lanes = pl.ds(pl.multiple_of(tile_of(place) * LANES, LANES), LANES)
        xs[pl.ds(place, rows, stride=SUBS), :] = x[:, lanes].astype(f32)
        cs[pl.ds(place, rows, stride=SUBS), :] = c[:, lanes].astype(f32)
        rates[pl.ds(place, modes, stride=SUBS), :] = rate[:, lanes]

    def row(ref, index):
        return ref[pl.ds(pl.multiple_of(index * SUBS, SUBS), SUBS), :]

    zero = jnp.zeros((SUBS, LANES), f32)

    def lag_step(block, sums):
        xv = [row(xs, block * SPAN + k) for k in range(SPAN)]
        cv = [row(cs, block * SPAN + k) for k in range(SPAN)]
        return tuple(
            sums[lag] + sum(cv[k] * xv[k - lag] for k in range(lag, SPAN)) for lag in range(SPAN)
        )

    lags = lax.fori_loop(0, blocks, lag_step, (zero,) * SPAN)
    for lag in range(SPAN):
        kept[pl.ds(2 * together * blocks * SUBS + lag * SUBS, SUBS), :] = lags[lag]

    def slot(mode, block, which):
        return pl.ds(pl.multiple_of(((mode * blocks + block) * 2 + which) * SUBS, SUBS), SUBS)

    def some_modes(group, carry):
        ids = [group * together + m for m in range(together)]
        decays = [row(rates, n) for n in ids]
        poles = [jnp.exp(-r) for r in decays]
        spans = [jnp.exp(-r * SPAN) for r in decays]
        slopes = [jnp.exp(-r * (SPAN - 1)) * SPAN for r in decays]

        def forward(block, state):
            xv = [row(xs, block * SPAN + k) for k in range(SPAN)]
            new = []
            for m in range(together):
                now, dnow = state[m]
                value, slope = horner(xv, poles[m])
                push = slope + slopes[m] * now
                kept[slot(m, block, 0), :] = now
                kept[slot(m, block, 1), :] = push
                new.append((now * spans[m] + value, dnow * spans[m] + push))
            return tuple(new)

        ends = lax.fori_loop(0, blocks, forward, ((zero, zero),) * together, unroll=True)

        def backward(index, state):
            block = blocks - 1 - index
            cv = [row(cs, block * SPAN + k) for k in reversed(range(SPAN))]
            new = []
            for m in range(together):
                now, dnow, first, second = state[m]
                value, slope = horner(cv, poles[m])
                entry = kept[slot(m, block, 0), :]
                push = kept[slot(m, block, 1), :]
                first = first + entry * value
                second = second + (entry * slope + now * push)
                new.append(
                    (
                        now * spans[m] + value,
                        dnow * spans[m] + (slope + slopes[m] * now),
                        first,
                        second,
                    )
                )
            return tuple(new)

        starts = lax.fori_loop(0, blocks, backward, ((zero,) * 4,) * together, unroll=True)
        lagged = [
            kept[pl.ds(2 * together * blocks * SUBS + lag * SUBS, SUBS), :]
            for lag in reversed(range(SPAN))
        ]
        for m in range(together):
            value, slope = horner(lagged, poles[m])
            first, second = starts[m][2:]
            results = (
                ends[m][0],
                starts[m][0],
                ends[m][1],
                starts[m][1],
                poles[m] * first + value,
                first + poles[m] * second + slope,
            )
            for part in range(PARTS):
                half = pl.ds((part * modes + ids[m]) * 4, 4)
                theirs[half, :] = results[part][:4]
                ours[half, :] = results[part][4:]
            our_rates[pl.ds(ids[m] * 4, 4), :] = decays[m][4:]
        return carry

    lax.fori_loop(0, modes // together, some_modes, 0)


def chip_tiles(away):
    def tile_of(place):
        chip, half, _ = position()
        return 8 * (place % 4) + 2 * (chip ^ away) + (half ^ (1 - place // 4))

    return tile_of


def next_tiles(first):
    return lambda place: first + place


def summary_parts(rows, modes, tile_of):
    together = 2
    kept = (2 * together * rows // SPAN + SPAN) * SUBS
    static = dict(tile_of=tile_of, rows=rows, modes=modes, together=together)
    shapes = [(PARTS * modes * 4, LANES), (PARTS * modes * 4, LANES), (modes * 4, LANES)]
    scratch = [(rows * SUBS, LANES), (rows * SUBS, LANES), (modes * SUBS, LANES), (kept, LANES)]
    return static, shapes, scratch


def summaries(inputs, cotangent, rate, tile_of, after=()):
    static, shapes, scratch = summary_parts(inputs.shape[0], rate.shape[0], tile_of)
    kernel = functools.partial(summary_kernel, **static)
    return local_call(
        kernel, "summaries", shapes, [inputs, cotangent, rate, *after], scratch, megabytes=4
    )


def first_summaries(inputs, cotangent, rate, residues, tile_of):
    static, shapes, scratch = summary_parts(inputs.shape[0], rate.shape[0], tile_of)
    operands = (inputs, cotangent, rate, residues)
    return pl.pallas_call(
        functools.partial(first_kernel, **static),
        in_specs=[far_away() for _ in operands],
        out_specs=[vmem() for _ in range(len(shapes) + 4)],
        out_shape=[pltpu.VMEM(shape, f32) for shape in shapes]
        + [pltpu.VMEM(item.shape, item.dtype) for item in operands],
        scratch_shapes=[pltpu.VMEM(shape, f32) for shape in scratch]
        + [pltpu.SemaphoreType.DMA((34,))],
        compiler_params=room(4),
        name="first_summaries",
    )(*[outside(item) for item in operands])


def joined(one, two, pole, power, slope):
    cross = one[END] * two[START]
    return (
        power * one[END] + two[END],
        one[START] + power * two[START],
        slope * one[END] + power * one[DEND] + two[DEND],
        one[DSTART] + slope * two[START] + power * two[DSTART],
        one[RES] + two[RES] + pole * cross,
        one[POLE] + two[POLE] + cross + pole * (one[DEND] * two[START] + one[END] * two[DSTART]),
    )


def pair_kernel(own, other, rates, *refs, level, rows, modes):
    send, hold = refs[-2:]
    size = modes * 4

    def body(one, two):
        r = rates[...]
        power = jnp.exp(-r * rows)
        slope = jnp.exp(-r * (rows - 1)) * float(rows)
        read = lambda ref: [ref[pl.ds(a * size, size), :] for a in range(PARTS)]
        second = read(two)
        result = joined(read(one), second, jnp.exp(-r), power, slope)
        for a in range(PARTS):
            send[pl.ds(a * size, size), :] = result[a]
        hold[pl.ds(0, size), :] = second[START]
        hold[pl.ds(size, size), :] = power

    later = bits()[level]

    @pl.when(later == 0)
    def _():
        body(own, other)

    @pl.when(later != 0)
    def _():
        body(other, own)


def paired(own, other, rates, level, rows, modes, after=()):
    return local_call(
        functools.partial(pair_kernel, level=level, rows=rows, modes=modes),
        "paired",
        [(PARTS * modes * 4, LANES), (2 * modes * 4, LANES)],
        [own, other, rates, *after],
    )


def close_kernel(own, other, rates, residues, *refs, modes, scale):
    term_keep, term_send, small, owned = refs
    chip, core, depth = position()
    size = modes * 4
    for q in range(4):
        lanes = pl.ds(pl.multiple_of((8 * q + 2 * chip + core) * LANES, LANES), LANES)
        small[pl.ds(q, modes, stride=4), :] = residues[:, lanes]
    pole = jnp.exp(-rates[...])
    later = chip // 2 != 0
    read = lambda ref, a: ref[pl.ds(a * size, size), :]
    pick = lambda a, one, two: jnp.where(later, read(two, a), read(one, a))
    now, dnow = pick(END, own, other), pick(DEND, own, other)
    start, dstart = pick(START, other, own), pick(DSTART, other, own)
    cross = now * start
    sum_res = read(own, RES) + read(other, RES) + pole * cross
    sum_pole = read(own, POLE) + read(other, POLE) + cross + pole * (dnow * start + now * dstart)
    owned[pl.ds(0, size), :] = sum_res * scale
    owned[pl.ds(size, size), :] = sum_pole * (-pole * small[...]) * scale
    for place in range(2):
        for ref, q in ((term_keep, 2 * place + depth % 2), (term_send, 2 * place + 1 - depth % 2)):
            for a in range(2):
                ref[pl.ds((place * 2 + a) * modes, modes), :] = owned[
                    pl.ds(a * size + q, modes, stride=4), :
                ]


def closed(own, other, rates, residues, scale):
    modes = residues.shape[0]
    size = modes * 4
    return local_call(
        functools.partial(close_kernel, modes=modes, scale=scale),
        "closed",
        [(4 * modes, LANES)] * 2,
        [own, other, rates, residues],
        [(size, LANES), (2 * size, LANES)],
    )


def hand_kernel(other, beside, hold_own, hold_side, *refs, modes):
    keep, send = refs[-2:]
    _, right, later = bits()
    size = modes * 4
    entering = (other[pl.ds(START * size, size), :], beside[...])
    for place, hold in enumerate((hold_own, hold_side)):
        rows_of = pl.ds(place * size, size)
        late = jnp.where(later == 0, entering[place], 0.0)
        early = hold[:size, :] + hold[size:, :] * late
        keep[rows_of, :] = jnp.where(right == 0, early, late)
        send[rows_of, :] = jnp.where(right == 0, late, early)


def handed(other, beside, hold_own, hold_side, modes, near):
    return local_call(
        functools.partial(hand_kernel, modes=modes),
        "handed",
        [(2 * modes * 4, LANES)] * 2,
        [other, beside, hold_own, hold_side, *near],
    )


def add_kernel(*refs, count):
    total = refs[0][...]
    for ref in refs[1:count]:
        total = total + ref[...]
    refs[-1][...] = total


def halve_kernel(kept, got, *refs):
    keep, send = refs[-2:]
    upper = position()[2] // 2
    half = kept.shape[0] // 2
    for ref, place in ((keep, upper), (send, 1 - upper)):
        at = pl.ds(pl.multiple_of(place * half, half), half)
        ref[...] = kept[at, :] + got[at, :]


def stack_kernel(one, two, *refs):
    out = refs[-1]
    half = out.shape[0] // 2
    out[:half, :] = one[-half:, :]
    out[half:, :] = two[-half:, :]


def stacked(one, two, rows, after=(), near=()):
    operands = [one, two, *near]
    return local_call(stack_kernel, "stacked", [(2 * rows, LANES)], operands, after=after)[0]


def entry_kernel(*refs, modes):
    kept, near = refs[:2]
    holds, (mine, theirs) = refs[2:6], refs[-2:]
    size = modes * 4
    backs = [kept[:size, :], near[:size, :], kept[size:, :], near[size:, :]]

    def body(late, early):
        for j in range(4):
            back = backs[j]
            late[pl.ds(j * size, size), :] = back
            early[pl.ds(j * size, size), :] = holds[j][:size, :] + holds[j][size:, :] * back

    core = position()[1]

    @pl.when(core == 0)
    def _():
        body(theirs, mine)

    @pl.when(core != 0)
    def _():
        body(mine, theirs)


def entries(kept, near, holds, modes, after):
    return local_call(
        functools.partial(entry_kernel, modes=modes),
        "entries",
        [(4 * modes * 4, LANES)] * 2,
        [kept, near, *holds, *after],
    )


def arranged(ref, scratch, block, height, change=None):
    for i in range(SUBS):
        tile = ref[:, pl.ds((block * SUBS + i) * LANES, LANES)].astype(f32)
        scratch[pl.ds(i, height, stride=SUBS), :] = tile if change is None else change(tile)


def mode_rows(ref, modes):
    return [ref[pl.ds(n * SUBS, SUBS), :] for n in range(modes)]


def tree_sum(terms):
    while len(terms) > 1:
        pairs = [a + b for a, b in zip(terms[::2], terms[1::2])]
        terms = pairs + ([terms[-1]] if len(terms) % 2 else [])
    return terms[0]


def slab_kernel(cot, rate, res, *refs, block, rows, modes):
    out, cs, ps, rs = refs[-4:]
    arranged(cot, cs, block, rows)
    arranged(rate, ps, block, modes, lambda tile: jnp.exp(-tile))
    arranged(res, rs, block, modes)
    poles, weights = mode_rows(ps, modes), mode_rows(rs, modes)

    def step(index, adjoint):
        now = pl.ds(pl.multiple_of((rows - 1 - index) * SUBS, SUBS), SUBS)
        value = cs[now, :]
        adjoint = tuple(a * p + value for a, p in zip(adjoint, poles))
        out[now, :] = tree_sum([a * w for a, w in zip(adjoint, weights)])
        return adjoint

    zero = jnp.zeros((SUBS, LANES), f32)
    lax.fori_loop(0, rows, step, (zero,) * modes, unroll=8)


def slab_gradients(cotangent, rate, residues, block, near=()):
    rows, modes = cotangent.shape[0], rate.shape[0]
    small = (modes * SUBS, LANES)
    return local_call(
        functools.partial(slab_kernel, block=block, rows=rows, modes=modes),
        "slab_gradients",
        [(rows * SUBS, LANES)],
        [cotangent, rate, residues, *near],
        [(rows * SUBS, LANES), small, small],
        megabytes=3,
    )[0]


def input_kernel(*refs, block, given, lead, own, fresh, rows, modes):
    refs = list(refs)
    take = lambda count: [refs.pop(0) for _ in range(count)]
    base, rate, res = take(3)
    entry, before = take(given), take(lead)
    done, ads, rs, ps, cs, ys, sent = [refs.pop() for _ in range(7)]
    whole = refs.pop() if lead or own else None
    width = SUBS * LANES
    copies = []

    def send(source, target):
        copies.append(pltpu.make_async_copy(source, target, done.at[len(copies)]))
        copies[-1].start()

    if lead:
        send(before[0], whole.at[:, pl.ds((block - 1) * width, width)])
    if fresh:
        arranged(base, cs, block, rows)
    arranged(rate, ps, block, modes, lambda tile: jnp.exp(-tile))
    arranged(res, rs, block, modes)
    if given == 1:
        arranged(entry[0], ads, block, modes)
    else:
        chip, half, _ = position()
        for j in range(4):
            for core, source in enumerate(entry):
                rows_of = pl.ds(j * modes * 4 + block, modes, stride=4)
                i = 2 * (chip ^ j) + (half ^ core)
                ads[pl.ds(i, modes, stride=SUBS), :] = source[rows_of, :]
    poles, weights = mode_rows(ps, modes), mode_rows(rs, modes)
    state = tuple(mode_rows(ads, modes))
    if not fresh:
        state = tuple(a * w for a, w in zip(state, weights))
    pieces = 4 if own else 1
    height = rows // pieces

    for piece in reversed(range(pieces)):

        def step(index, state):
            position_in = (piece + 1) * height - 1 - index
            now = pl.ds(pl.multiple_of(position_in * SUBS, SUBS), SUBS)
            if fresh:
                value = cs[now, :]
                state = tuple(a * p + value for a, p in zip(state, poles))
                ys[now, :] = tree_sum([a * w for a, w in zip(state, weights)])
            else:
                state = tuple(a * p for a, p in zip(state, poles))
                ys[now, :] = base[now, :] + tree_sum(list(state))
            return state

        state = lax.fori_loop(0, height, step, state, unroll=8)
        span = pl.ds(piece * height, height)
        for i in range(SUBS):
            tile = ys[pl.ds(piece * height * SUBS + i, height, stride=SUBS), :].astype(sent.dtype)
            sent[span, pl.ds(i * LANES, LANES)] = tile
        if own:
            send(sent.at[span], whole.at[span, pl.ds(block * width, width)])
    for copy in copies:
        copy.wait()


def far_away():
    return pl.BlockSpec(memory_space=pltpu.HBM)


def outside(value):
    return pltpu.with_memory_space_constraint(value, pltpu.HBM)


def input_gradients(cotangent, rate, residues, given, block, lead=None, onto=None, own=False, slab=None):
    rows, channels = cotangent.shape
    modes, dtype = rate.shape[0], cotangent.dtype
    width = SUBS * LANES
    base = cotangent if slab is None else slab
    small = pltpu.VMEM((modes * SUBS, LANES), f32)
    operands = [base, rate, residues, *given, *([] if lead is None else [lead])]
    operands = [here(item) for item in operands]
    in_specs = [vmem() for _ in operands]
    shapes, specs, aliases = [], [], {}
    if lead is not None or own:
        shapes.append(jax.ShapeDtypeStruct((rows, channels), dtype))
        specs.append(far_away())
    if onto is not None:
        aliases = {len(operands): 0}
        operands.append(outside(onto))
        in_specs.append(far_away())
    shapes.append(pltpu.VMEM((rows, width), dtype))
    specs.append(vmem())
    return pl.pallas_call(
        functools.partial(
            input_kernel,
            block=block,
            given=len(given),
            lead=int(lead is not None),
            own=own,
            fresh=slab is None,
            rows=rows,
            modes=modes,
        ),
        in_specs=in_specs,
        out_specs=specs,
        out_shape=shapes,
        scratch_shapes=[pltpu.VMEM((rows * SUBS, LANES), f32)] * 2
        + [small, small, small, pltpu.SemaphoreType.DMA((5,))],
        input_output_aliases=aliases,
        compiler_params=room(3),
        name="input_gradients",
    )(*operands)


def place_kernel(*refs, modes):
    pieces, (out_res, out_rate) = refs[:2], refs[-2:]
    chip, half, _ = position()
    for j in range(4):
        for core in range(2):
            i = 2 * (chip ^ j) + (half ^ core)
            lanes = pl.ds(pl.multiple_of(i * LANES, LANES), LANES)
            row = ((j % 2) * 2 + core) * 2 * modes
            out_res[:, lanes] = pieces[j // 2][pl.ds(row, modes), :]
            out_rate[:, lanes] = pieces[j // 2][pl.ds(row + modes, modes), :]


def placed(pieces, modes, after):
    shape = jax.ShapeDtypeStruct((modes, SUBS * LANES), f32)
    return pl.pallas_call(
        functools.partial(place_kernel, modes=modes),
        in_specs=[vmem() for _ in pieces] + [far_away()],
        out_specs=[vmem(), vmem()],
        out_shape=[shape, shape],
        compiler_params=room(2),
        name="placed",
    )(
        *[here(item) for item in pieces],
        outside(after),
    )


def crossed(value, distance):
    return lax.ppermute(value, "context", [(i, i ^ distance) for i in range(8)])


def shifted(value, distance):
    return lax.ppermute(value, "dp", [(i, i ^ distance) for i in range(4)])


def four_by_eight(inputs, cotangent, rate, residues):
    x, c = inputs[0], cotangent[0]
    rows, modes = x.shape[0], rate.shape[0]
    theirs, ours, rates, x, c, rate, residues = first_summaries(
        x, c, rate, residues, chip_tiles(ORDER[0])
    )
    holds = {}

    def cores(away, ours, others, rates, after=()):
        sums, holds[away] = paired(ours, others, rates, 0, rows, modes, after)
        return sums

    def more(away, after=()):
        theirs, ours, rates = summaries(x, c, rate, chip_tiles(away), after)
        return crossed(theirs, 1), ours, rates

    theirs3 = crossed(theirs, 1)
    theirs1, ours1, rates1 = more(1)
    got2 = crossed(cores(3, ours, theirs3, rates, (rates1,)), 2)
    theirs2, ours2, rates2 = more(2, (holds[3],))
    got0 = crossed(cores(1, ours1, theirs1, rates1, (rates2,)), 2)
    slab = functools.partial(slab_gradients, c, rate, residues)
    landed = stacked(got2, holds[1], 8)
    row2 = cores(2, ours2, theirs2, rates2, (landed,))
    row2, hold_side = paired(row2, got2, rates2, 1, 2 * rows, modes)
    other = crossed(row2, 4)
    theirs0, ours0, rates0 = more(0, (hold_side, holds[1]))
    landed = stacked(stacked(other, rates0, 8), got0, 8)
    row0 = cores(0, ours0, theirs0, rates0, (landed,))
    row0, hold_own = paired(row0, got0, rates0, 1, 2 * rows, modes)
    beside = crossed(row0[START * 4 * modes : (START + 1) * 4 * modes], 4)
    scale = 1.0 / math.sqrt(4 * rows * 8)
    term_keep, term_send = closed(row0, other, rates0, residues, scale)
    half = (2 * modes, LANES)
    slab2 = slab(2, (term_keep,))
    keep, send = local_call(
        halve_kernel, "halved", [half, half], [term_keep, shifted(term_send, 1), slab2]
    )
    back_keep, back_send = handed(other, beside, hold_own, hold_side, modes, (send,))
    back_near = crossed(back_send, 2)
    slab3 = slab(3, (back_keep,))
    (total,) = local_call(
        functools.partial(add_kernel, count=2), "added", [half], [keep, shifted(send, 2), slab3]
    )
    mine, others = entries(back_keep, back_near, [holds[j] for j in range(4)], modes, (total,))
    entry = (mine, crossed(others, 1))
    both = stacked(total, crossed(total, 1), 2 * modes)
    gradients = functools.partial(input_gradients, c, rate, residues, entry)
    (part0,) = gradients(0)
    grad_inputs, part1 = gradients(1, part0)
    four = stacked(both, crossed(both, 2), 4 * modes, (), (part1,))
    grad_inputs, part2 = gradients(2, part1, grad_inputs, False, slab2)
    grad_inputs, _ = gradients(3, part2, grad_inputs, True, slab3)
    grad_residues, grad_rate = placed([four, crossed(four, 4)], modes, grad_inputs)
    return (grad_inputs[None], grad_residues, grad_rate)


def any_mesh(inputs, cotangent, rate, residues):
    x, c = inputs[0], cotangent[0]
    rows, channels, modes = x.shape[0], x.shape[1], rate.shape[0]
    slab_count, mine = lax.axis_size("context"), lax.axis_index("context")
    blocks = [
        summaries(x, c, rate, next_tiles(first))[:2] for first in range(0, channels // LANES, SUBS)
    ]
    local = jnp.stack([half for pair in blocks for half in pair])
    local = local.reshape(-1, PARTS, modes, 4 * LANES)
    local = jnp.moveaxis(local, 0, 2).reshape(PARTS, modes, channels)
    slabs = lax.all_gather(local, "context")
    pole, power = jnp.exp(-rate), jnp.exp(-rate * rows)
    slope = jnp.exp(-rate * (rows - 1)) * rows
    total = tuple(slabs[0])
    for place in range(1, slab_count):
        total = joined(total, slabs[place], pole, power, slope)
    zero = jnp.zeros_like(pole)

    def behind(index, entry):
        place = slab_count - 1 - index
        return jnp.where(place > mine, slabs[place, START] + power * entry, entry)

    entry = lax.fori_loop(0, slab_count, behind, zero)
    count = channels // (SUBS * LANES)
    lead = grad_inputs = None
    for block in range(count):
        last = block == count - 1
        *grad_inputs, lead = input_gradients(
            c, rate, residues, [entry], block, lead, grad_inputs, last
        )
        grad_inputs = grad_inputs[0] if grad_inputs else None
    scale = 1.0 / math.sqrt(lax.axis_size("dp") * rows * slab_count)
    terms = jnp.stack([total[RES], total[POLE] * (-pole * residues)]) * scale
    owned = lax.psum_scatter(terms, "dp", scatter_dimension=2, tiled=True)
    return (grad_inputs[None], owned[0], owned[1])


def solution(mesh):
    tuned = mesh.shape["dp"] == 4 and mesh.shape["context"] == 8
    in_specs = (P("dp", "context", None), P("dp", "context", None), P(), P())
    out_specs = (P("dp", "context", None), P(None, "dp"), P(None, "dp"))
    return jax.shard_map(
        four_by_eight if tuned else any_mesh, mesh=mesh, in_specs=in_specs, out_specs=out_specs, check_vma=False
    )
```

```python
import functools
import math

import jax
import jax.numpy as jnp
from jax import lax
from jax.experimental import pallas as pl
from jax.experimental.pallas import tpu as pltpu
from jax.sharding import PartitionSpec as P

LANES = 128
SUBS = 8
SPAN = 8
PARTS = 6
ORDER = (3, 1, 2, 0)
END, START, DEND, DSTART, RES, POLE = range(PARTS)
f32 = jnp.float32


def here(value):
    return pltpu.with_memory_space_constraint(value, pltpu.VMEM)


def vmem():
    return pl.BlockSpec(memory_space=pltpu.VMEM)


def position():
    context = lax.axis_index("context")
    return context // 2, context % 2, lax.axis_index("dp")


def room(megabytes):
    return pltpu.CompilerParams(vmem_limit_bytes=megabytes << 20)


def bits():
    chip, core, _ = position()
    return core, chip % 2, chip // 2


def local_call(kernel, name, shapes, operands, scratch=(), megabytes=2, after=()):
    return pl.pallas_call(
        kernel,
        in_specs=[vmem() for _ in operands] + [far_away() for _ in after],
        out_specs=[vmem() for _ in shapes],
        out_shape=[pltpu.VMEM(shape, f32) for shape in shapes],
        scratch_shapes=[pltpu.VMEM(shape, f32) for shape in scratch],
        compiler_params=room(megabytes),
        name=name,
    )(*[here(item) for item in operands], *[outside(item) for item in after])


def horner(values, point):
    value, slope, scaled = values[0], None, None
    for item in values[1:]:
        if slope is None:
            slope = value
        elif scaled is not None and slope is values[0]:
            slope = scaled + value
        else:
            slope = slope * point + value
        scaled = value * point
        value = scaled + item
    return value, slope


def spread(tiles, scratch, rows, stride):
    for place, tile in enumerate(tiles):
        scratch[pl.ds(place, rows, stride=stride), :] = tile


def summary_kernel(x, c, rate, *refs, **static):
    summarize(x, c, rate, *refs[-7:], **static)


def first_kernel(*refs, **static):
    x, c, rate, res, *outs, x_in, c_in, rate_in, res_in, xs, cs, held, kept, done = refs
    chip, _, _ = position()
    half = 4 * LANES
    copies = [(rate, rate_in)]

    def tiles(away, width):
        for q in range(4):
            first = (chip ^ away) * 2 * LANES // width * width
            lanes = pl.ds(pl.multiple_of(8 * LANES * q + first, width), width)
            pairs = ((x, x_in), (c, c_in))
            copies.extend((ref.at[:, lanes], into.at[:, lanes]) for ref, into in pairs)

    tiles(3, half // 2)
    ahead = len(copies)
    tiles(2, half // 2)
    tiles(0, half)
    copies.append((res, res_in))
    copies = [
        pltpu.make_async_copy(source, into, done.at[place])
        for place, (source, into) in enumerate(copies)
    ]
    for copy in copies[:ahead]:
        copy.start()
    for copy in copies[:ahead]:
        copy.wait()
    for copy in copies[ahead:]:
        copy.start()
    summarize(x_in, c_in, rate_in, *outs, xs, cs, held, kept, **static)
    for copy in copies[ahead:]:
        copy.wait()


def summarize(x, c, rate, theirs, ours, our_rates, xs, cs, rates, kept, *, tile_of, rows, modes, together):
    blocks = rows // SPAN
    for place in range(SUBS):
        lanes = pl.ds(pl.multiple_of(tile_of(place) * LANES, LANES), LANES)
        xs[pl.ds(place, rows, stride=SUBS), :] = x[:, lanes].astype(f32)
        cs[pl.ds(place, rows, stride=SUBS), :] = c[:, lanes].astype(f32)
        rates[pl.ds(place, modes, stride=SUBS), :] = rate[:, lanes]

    def row(ref, index):
        return ref[pl.ds(pl.multiple_of(index * SUBS, SUBS), SUBS), :]

    zero = jnp.zeros((SUBS, LANES), f32)

    def lag_step(block, sums):
        xv = [row(xs, block * SPAN + k) for k in range(SPAN)]
        cv = [row(cs, block * SPAN + k) for k in range(SPAN)]
        return tuple(
            sums[lag] + sum(cv[k] * xv[k - lag] for k in range(lag, SPAN)) for lag in range(SPAN)
        )

    lags = lax.fori_loop(0, blocks, lag_step, (zero,) * SPAN)
    for lag in range(SPAN):
        kept[pl.ds(2 * together * blocks * SUBS + lag * SUBS, SUBS), :] = lags[lag]

    def slot(mode, block, which):
        return pl.ds(pl.multiple_of(((mode * blocks + block) * 2 + which) * SUBS, SUBS), SUBS)

    def some_modes(group, carry):
        ids = [group * together + m for m in range(together)]
        decays = [row(rates, n) for n in ids]
        poles = [jnp.exp(-r) for r in decays]
        spans = [jnp.exp(-r * SPAN) for r in decays]
        slopes = [jnp.exp(-r * (SPAN - 1)) * SPAN for r in decays]

        def forward(block, state):
            xv = [row(xs, block * SPAN + k) for k in range(SPAN)]
            new = []
            for m in range(together):
                now, dnow = state[m]
                value, slope = horner(xv, poles[m])
                push = slope + slopes[m] * now
                kept[slot(m, block, 0), :] = now
                kept[slot(m, block, 1), :] = push
                new.append((now * spans[m] + value, dnow * spans[m] + push))
            return tuple(new)

        ends = lax.fori_loop(0, blocks, forward, ((zero, zero),) * together, unroll=True)

        def backward(index, state):
            block = blocks - 1 - index
            cv = [row(cs, block * SPAN + k) for k in reversed(range(SPAN))]
            new = []
            for m in range(together):
                now, dnow, first, second = state[m]
                value, slope = horner(cv, poles[m])
                entry = kept[slot(m, block, 0), :]
                push = kept[slot(m, block, 1), :]
                first = first + entry * value
                second = second + (entry * slope + now * push)
                new.append(
                    (
                        now * spans[m] + value,
                        dnow * spans[m] + (slope + slopes[m] * now),
                        first,
                        second,
                    )
                )
            return tuple(new)

        starts = lax.fori_loop(0, blocks, backward, ((zero,) * 4,) * together, unroll=True)
        lagged = [
            kept[pl.ds(2 * together * blocks * SUBS + lag * SUBS, SUBS), :]
            for lag in reversed(range(SPAN))
        ]
        for m in range(together):
            value, slope = horner(lagged, poles[m])
            first, second = starts[m][2:]
            results = (
                ends[m][0],
                starts[m][0],
                ends[m][1],
                starts[m][1],
                poles[m] * first + value,
                first + poles[m] * second + slope,
            )
            for part in range(PARTS):
                half = pl.ds((part * modes + ids[m]) * 4, 4)
                theirs[half, :] = results[part][:4]
                ours[half, :] = results[part][4:]
            our_rates[pl.ds(ids[m] * 4, 4), :] = decays[m][4:]
        return carry

    lax.fori_loop(0, modes // together, some_modes, 0)


def chip_tiles(away):
    def tile_of(place):
        chip, half, _ = position()
        return 8 * (place % 4) + 2 * (chip ^ away) + (half ^ (1 - place // 4))

    return tile_of


def next_tiles(first):
    return lambda place: first + place


def summary_parts(rows, modes, tile_of):
    together = 2
    kept = (2 * together * rows // SPAN + SPAN) * SUBS
    static = dict(tile_of=tile_of, rows=rows, modes=modes, together=together)
    shapes = [(PARTS * modes * 4, LANES), (PARTS * modes * 4, LANES), (modes * 4, LANES)]
    scratch = [(rows * SUBS, LANES), (rows * SUBS, LANES), (modes * SUBS, LANES), (kept, LANES)]
    return static, shapes, scratch


def summaries(inputs, cotangent, rate, tile_of, after=()):
    static, shapes, scratch = summary_parts(inputs.shape[0], rate.shape[0], tile_of)
    kernel = functools.partial(summary_kernel, **static)
    return local_call(
        kernel, "summaries", shapes, [inputs, cotangent, rate, *after], scratch, megabytes=4
    )


def first_summaries(inputs, cotangent, rate, residues, tile_of):
    static, shapes, scratch = summary_parts(inputs.shape[0], rate.shape[0], tile_of)
    operands = (inputs, cotangent, rate, residues)
    return pl.pallas_call(
        functools.partial(first_kernel, **static),
        in_specs=[far_away() for _ in operands],
        out_specs=[vmem() for _ in range(len(shapes) + 4)],
        out_shape=[pltpu.VMEM(shape, f32) for shape in shapes]
        + [pltpu.VMEM(item.shape, item.dtype) for item in operands],
        scratch_shapes=[pltpu.VMEM(shape, f32) for shape in scratch]
        + [pltpu.SemaphoreType.DMA((26,))],
        compiler_params=room(4),
        name="first_summaries",
    )(*[outside(item) for item in operands])


def joined(one, two, pole, power, slope):
    cross = one[END] * two[START]
    return (
        power * one[END] + two[END],
        one[START] + power * two[START],
        slope * one[END] + power * one[DEND] + two[DEND],
        one[DSTART] + slope * two[START] + power * two[DSTART],
        one[RES] + two[RES] + pole * cross,
        one[POLE] + two[POLE] + cross + pole * (one[DEND] * two[START] + one[END] * two[DSTART]),
    )


def pair_kernel(own, other, rates, *refs, level, rows, modes):
    send, hold = refs[-2:]
    size = modes * 4

    def body(one, two):
        r = rates[...]
        power = jnp.exp(-r * rows)
        slope = jnp.exp(-r * (rows - 1)) * float(rows)
        read = lambda ref: [ref[pl.ds(a * size, size), :] for a in range(PARTS)]
        second = read(two)
        result = joined(read(one), second, jnp.exp(-r), power, slope)
        for a in range(PARTS):
            send[pl.ds(a * size, size), :] = result[a]
        hold[pl.ds(0, size), :] = second[START]
        hold[pl.ds(size, size), :] = power

    later = bits()[level]

    @pl.when(later == 0)
    def _():
        body(own, other)

    @pl.when(later != 0)
    def _():
        body(other, own)


def paired(own, other, rates, level, rows, modes, after=()):
    return local_call(
        functools.partial(pair_kernel, level=level, rows=rows, modes=modes),
        "paired",
        [(PARTS * modes * 4, LANES), (2 * modes * 4, LANES)],
        [own, other, rates, *after],
    )


def close_kernel(own, other, rates, residues, *refs, modes, scale):
    term_keep, term_send, small, owned = refs
    chip, core, depth = position()
    size = modes * 4
    for q in range(4):
        lanes = pl.ds(pl.multiple_of((8 * q + 2 * chip + core) * LANES, LANES), LANES)
        small[pl.ds(q, modes, stride=4), :] = residues[:, lanes]
    pole = jnp.exp(-rates[...])
    later = chip // 2 != 0
    read = lambda ref, a: ref[pl.ds(a * size, size), :]
    pick = lambda a, one, two: jnp.where(later, read(two, a), read(one, a))
    now, dnow = pick(END, own, other), pick(DEND, own, other)
    start, dstart = pick(START, other, own), pick(DSTART, other, own)
    cross = now * start
    sum_res = read(own, RES) + read(other, RES) + pole * cross
    sum_pole = read(own, POLE) + read(other, POLE) + cross + pole * (dnow * start + now * dstart)
    owned[pl.ds(0, size), :] = sum_res * scale
    owned[pl.ds(size, size), :] = sum_pole * (-pole * small[...]) * scale
    for place in range(2):
        for ref, q in ((term_keep, 2 * place + depth % 2), (term_send, 2 * place + 1 - depth % 2)):
            for a in range(2):
                ref[pl.ds((place * 2 + a) * modes, modes), :] = owned[
                    pl.ds(a * size + q, modes, stride=4), :
                ]


def closed(own, other, rates, residues, scale):
    modes = residues.shape[0]
    size = modes * 4
    return local_call(
        functools.partial(close_kernel, modes=modes, scale=scale),
        "closed",
        [(4 * modes, LANES)] * 2,
        [own, other, rates, residues],
        [(size, LANES), (2 * size, LANES)],
    )


def hand_kernel(other, beside, hold_own, hold_side, *refs, modes):
    keep, send = refs[-2:]
    _, right, later = bits()
    size = modes * 4
    entering = (other[pl.ds(START * size, size), :], beside[...])
    for place, hold in enumerate((hold_own, hold_side)):
        rows_of = pl.ds(place * size, size)
        late = jnp.where(later == 0, entering[place], 0.0)
        early = hold[:size, :] + hold[size:, :] * late
        keep[rows_of, :] = jnp.where(right == 0, early, late)
        send[rows_of, :] = jnp.where(right == 0, late, early)


def handed(other, beside, hold_own, hold_side, modes, near):
    return local_call(
        functools.partial(hand_kernel, modes=modes),
        "handed",
        [(2 * modes * 4, LANES)] * 2,
        [other, beside, hold_own, hold_side, *near],
    )


def add_kernel(*refs, count):
    total = refs[0][...]
    for ref in refs[1:count]:
        total = total + ref[...]
    refs[-1][...] = total


def halve_kernel(kept, got, *refs):
    keep, send = refs[-2:]
    upper = position()[2] // 2
    half = kept.shape[0] // 2
    for ref, place in ((keep, upper), (send, 1 - upper)):
        at = pl.ds(pl.multiple_of(place * half, half), half)
        ref[...] = kept[at, :] + got[at, :]


def stack_kernel(one, two, *refs):
    out = refs[-1]
    half = out.shape[0] // 2
    out[:half, :] = one[-half:, :]
    out[half:, :] = two[-half:, :]


def stacked(one, two, rows, after=(), near=()):
    operands = [one, two, *near]
    return local_call(stack_kernel, "stacked", [(2 * rows, LANES)], operands, after=after)[0]


def entry_kernel(*refs, modes):
    kept, near = refs[:2]
    holds, (mine, theirs) = refs[2:6], refs[-2:]
    size = modes * 4
    backs = [kept[:size, :], near[:size, :], kept[size:, :], near[size:, :]]

    def body(late, early):
        for j in range(4):
            back = backs[j]
            late[pl.ds(j * size, size), :] = back
            early[pl.ds(j * size, size), :] = holds[j][:size, :] + holds[j][size:, :] * back

    core = position()[1]

    @pl.when(core == 0)
    def _():
        body(theirs, mine)

    @pl.when(core != 0)
    def _():
        body(mine, theirs)


def entries(kept, near, holds, modes, after):
    return local_call(
        functools.partial(entry_kernel, modes=modes),
        "entries",
        [(4 * modes * 4, LANES)] * 2,
        [kept, near, *holds, *after],
    )


def arranged(ref, scratch, block, height, change=None):
    for i in range(SUBS):
        tile = ref[:, pl.ds((block * SUBS + i) * LANES, LANES)].astype(f32)
        scratch[pl.ds(i, height, stride=SUBS), :] = tile if change is None else change(tile)


def mode_rows(ref, modes):
    return [ref[pl.ds(n * SUBS, SUBS), :] for n in range(modes)]


def tree_sum(terms):
    while len(terms) > 1:
        pairs = [a + b for a, b in zip(terms[::2], terms[1::2])]
        terms = pairs + ([terms[-1]] if len(terms) % 2 else [])
    return terms[0]


def slab_kernel(cot, rate, res, *refs, block, rows, modes):
    out, cs, ps, rs = refs[-4:]
    arranged(cot, cs, block, rows)
    arranged(rate, ps, block, modes, lambda tile: jnp.exp(-tile))
    arranged(res, rs, block, modes)
    poles, weights = mode_rows(ps, modes), mode_rows(rs, modes)

    def step(index, adjoint):
        now = pl.ds(pl.multiple_of((rows - 1 - index) * SUBS, SUBS), SUBS)
        value = cs[now, :]
        adjoint = tuple(a * p + value for a, p in zip(adjoint, poles))
        out[now, :] = tree_sum([a * w for a, w in zip(adjoint, weights)])
        return adjoint

    zero = jnp.zeros((SUBS, LANES), f32)
    lax.fori_loop(0, rows, step, (zero,) * modes, unroll=8)


def slab_gradients(cotangent, rate, residues, block, near=()):
    rows, modes = cotangent.shape[0], rate.shape[0]
    small = (modes * SUBS, LANES)
    return local_call(
        functools.partial(slab_kernel, block=block, rows=rows, modes=modes),
        "slab_gradients",
        [(rows * SUBS, LANES)],
        [cotangent, rate, residues, *near],
        [(rows * SUBS, LANES), small, small],
        megabytes=3,
    )[0]


def input_kernel(*refs, block, given, lead, own, fresh, rows, modes):
    refs = list(refs)
    take = lambda count: [refs.pop(0) for _ in range(count)]
    base, rate, res = take(3)
    entry, before = take(given), take(lead)
    done, ads, rs, ps, cs, ys, sent = [refs.pop() for _ in range(7)]
    whole = refs.pop() if lead or own else None
    width = SUBS * LANES
    copies = []

    def send(source, target):
        copies.append(pltpu.make_async_copy(source, target, done.at[len(copies)]))
        copies[-1].start()

    if lead:
        send(before[0], whole.at[:, pl.ds((block - 1) * width, width)])
    if fresh:
        arranged(base, cs, block, rows)
    arranged(rate, ps, block, modes, lambda tile: jnp.exp(-tile))
    arranged(res, rs, block, modes)
    if given == 1:
        arranged(entry[0], ads, block, modes)
    else:
        chip, half, _ = position()
        for j in range(4):
            for core, source in enumerate(entry):
                rows_of = pl.ds(j * modes * 4 + block, modes, stride=4)
                i = 2 * (chip ^ j) + (half ^ core)
                ads[pl.ds(i, modes, stride=SUBS), :] = source[rows_of, :]
    poles, weights = mode_rows(ps, modes), mode_rows(rs, modes)
    state = tuple(mode_rows(ads, modes))
    if not fresh:
        state = tuple(a * w for a, w in zip(state, weights))
    pieces = 4 if own else 1
    height = rows // pieces

    for piece in reversed(range(pieces)):

        def step(index, state):
            position_in = (piece + 1) * height - 1 - index
            now = pl.ds(pl.multiple_of(position_in * SUBS, SUBS), SUBS)
            if fresh:
                value = cs[now, :]
                state = tuple(a * p + value for a, p in zip(state, poles))
                ys[now, :] = tree_sum([a * w for a, w in zip(state, weights)])
            else:
                state = tuple(a * p for a, p in zip(state, poles))
                ys[now, :] = base[now, :] + tree_sum(list(state))
            return state

        state = lax.fori_loop(0, height, step, state, unroll=8)
        span = pl.ds(piece * height, height)
        for i in range(SUBS):
            tile = ys[pl.ds(piece * height * SUBS + i, height, stride=SUBS), :].astype(sent.dtype)
            sent[span, pl.ds(i * LANES, LANES)] = tile
        if own:
            send(sent.at[span], whole.at[span, pl.ds(block * width, width)])
    for copy in copies:
        copy.wait()


def far_away():
    return pl.BlockSpec(memory_space=pltpu.HBM)


def outside(value):
    return pltpu.with_memory_space_constraint(value, pltpu.HBM)


def input_gradients(cotangent, rate, residues, given, block, lead=None, onto=None, own=False, slab=None):
    rows, channels = cotangent.shape
    modes, dtype = rate.shape[0], cotangent.dtype
    width = SUBS * LANES
    base = cotangent if slab is None else slab
    small = pltpu.VMEM((modes * SUBS, LANES), f32)
    operands = [base, rate, residues, *given, *([] if lead is None else [lead])]
    operands = [here(item) for item in operands]
    in_specs = [vmem() for _ in operands]
    shapes, specs, aliases = [], [], {}
    if lead is not None or own:
        shapes.append(jax.ShapeDtypeStruct((rows, channels), dtype))
        specs.append(far_away())
    if onto is not None:
        aliases = {len(operands): 0}
        operands.append(outside(onto))
        in_specs.append(far_away())
    shapes.append(pltpu.VMEM((rows, width), dtype))
    specs.append(vmem())
    return pl.pallas_call(
        functools.partial(
            input_kernel,
            block=block,
            given=len(given),
            lead=int(lead is not None),
            own=own,
            fresh=slab is None,
            rows=rows,
            modes=modes,
        ),
        in_specs=in_specs,
        out_specs=specs,
        out_shape=shapes,
        scratch_shapes=[pltpu.VMEM((rows * SUBS, LANES), f32)] * 2
        + [small, small, small, pltpu.SemaphoreType.DMA((5,))],
        input_output_aliases=aliases,
        compiler_params=room(3),
        name="input_gradients",
    )(*operands)


def place_kernel(*refs, modes):
    pieces, (out_res, out_rate) = refs[:2], refs[-2:]
    chip, half, _ = position()
    for j in range(4):
        for core in range(2):
            i = 2 * (chip ^ j) + (half ^ core)
            lanes = pl.ds(pl.multiple_of(i * LANES, LANES), LANES)
            row = ((j % 2) * 2 + core) * 2 * modes
            out_res[:, lanes] = pieces[j // 2][pl.ds(row, modes), :]
            out_rate[:, lanes] = pieces[j // 2][pl.ds(row + modes, modes), :]


def placed(pieces, modes, after):
    shape = jax.ShapeDtypeStruct((modes, SUBS * LANES), f32)
    return pl.pallas_call(
        functools.partial(place_kernel, modes=modes),
        in_specs=[vmem() for _ in pieces] + [far_away()],
        out_specs=[vmem(), vmem()],
        out_shape=[shape, shape],
        compiler_params=room(2),
        name="placed",
    )(
        *[here(item) for item in pieces],
        outside(after),
    )


def crossed(value, distance):
    return lax.ppermute(value, "context", [(i, i ^ distance) for i in range(8)])


def shifted(value, distance):
    return lax.ppermute(value, "dp", [(i, i ^ distance) for i in range(4)])


def four_by_eight(inputs, cotangent, rate, residues):
    x, c = inputs[0], cotangent[0]
    rows, modes = x.shape[0], rate.shape[0]
    theirs, ours, rates, x, c, rate, residues = first_summaries(
        x, c, rate, residues, chip_tiles(ORDER[0])
    )
    holds = {}

    def cores(away, ours, others, rates, after=()):
        sums, holds[away] = paired(ours, others, rates, 0, rows, modes, after)
        return sums

    def more(away, after=()):
        theirs, ours, rates = summaries(x, c, rate, chip_tiles(away), after)
        return crossed(theirs, 1), ours, rates

    theirs3 = crossed(theirs, 1)
    theirs1, ours1, rates1 = more(1)
    got2 = crossed(cores(3, ours, theirs3, rates, (rates1,)), 2)
    theirs2, ours2, rates2 = more(2, (holds[3],))
    got0 = crossed(cores(1, ours1, theirs1, rates1, (rates2,)), 2)
    slab = functools.partial(slab_gradients, c, rate, residues)
    landed = stacked(got2, holds[1], 8)
    row2 = cores(2, ours2, theirs2, rates2, (landed,))
    row2, hold_side = paired(row2, got2, rates2, 1, 2 * rows, modes)
    other = crossed(row2, 4)
    theirs0, ours0, rates0 = more(0, (hold_side, holds[1]))
    landed = stacked(other, got0, 8)
    row0 = cores(0, ours0, theirs0, rates0, (landed,))
    row0, hold_own = paired(row0, got0, rates0, 1, 2 * rows, modes)
    beside = crossed(row0[START * 4 * modes : (START + 1) * 4 * modes], 4)
    scale = 1.0 / math.sqrt(4 * rows * 8)
    term_keep, term_send = closed(row0, other, rates0, residues, scale)
    half = (2 * modes, LANES)
    slab2 = slab(2, (term_keep,))
    keep, send = local_call(
        halve_kernel, "halved", [half, half], [term_keep, shifted(term_send, 1), slab2]
    )
    back_keep, back_send = handed(other, beside, hold_own, hold_side, modes, (send,))
    back_near = crossed(back_send, 2)
    slab3 = slab(3, (back_keep,))
    (total,) = local_call(
        functools.partial(add_kernel, count=2), "added", [half], [keep, shifted(send, 2), slab3]
    )
    mine, others = entries(back_keep, back_near, [holds[j] for j in range(4)], modes, (total,))
    entry = (mine, crossed(others, 1))
    both = stacked(total, crossed(total, 1), 2 * modes)
    gradients = functools.partial(input_gradients, c, rate, residues, entry)
    (part0,) = gradients(0)
    grad_inputs, part1 = gradients(1, part0)
    four = stacked(both, crossed(both, 2), 4 * modes, (), (part1,))
    grad_inputs, part2 = gradients(2, part1, grad_inputs, False, slab2)
    grad_inputs, _ = gradients(3, part2, grad_inputs, True, slab3)
    grad_residues, grad_rate = placed([four, crossed(four, 4)], modes, grad_inputs)
    return (grad_inputs[None], grad_residues, grad_rate)


def any_mesh(inputs, cotangent, rate, residues):
    x, c = inputs[0], cotangent[0]
    rows, channels, modes = x.shape[0], x.shape[1], rate.shape[0]
    slab_count, mine = lax.axis_size("context"), lax.axis_index("context")
    blocks = [
        summaries(x, c, rate, next_tiles(first))[:2] for first in range(0, channels // LANES, SUBS)
    ]
    local = jnp.stack([half for pair in blocks for half in pair])
    local = local.reshape(-1, PARTS, modes, 4 * LANES)
    local = jnp.moveaxis(local, 0, 2).reshape(PARTS, modes, channels)
    slabs = lax.all_gather(local, "context")
    pole, power = jnp.exp(-rate), jnp.exp(-rate * rows)
    slope = jnp.exp(-rate * (rows - 1)) * rows
    total = tuple(slabs[0])
    for place in range(1, slab_count):
        total = joined(total, slabs[place], pole, power, slope)
    zero = jnp.zeros_like(pole)

    def behind(index, entry):
        place = slab_count - 1 - index
        return jnp.where(place > mine, slabs[place, START] + power * entry, entry)

    entry = lax.fori_loop(0, slab_count, behind, zero)
    count = channels // (SUBS * LANES)
    lead = grad_inputs = None
    for block in range(count):
        last = block == count - 1
        *grad_inputs, lead = input_gradients(
            c, rate, residues, [entry], block, lead, grad_inputs, last
        )
        grad_inputs = grad_inputs[0] if grad_inputs else None
    scale = 1.0 / math.sqrt(lax.axis_size("dp") * rows * slab_count)
    terms = jnp.stack([total[RES], total[POLE] * (-pole * residues)]) * scale
    owned = lax.psum_scatter(terms, "dp", scatter_dimension=2, tiled=True)
    return (grad_inputs[None], owned[0], owned[1])


def solution(mesh):
    tuned = mesh.shape["dp"] == 4 and mesh.shape["context"] == 8
    in_specs = (P("dp", "context", None), P("dp", "context", None), P(), P())
    out_specs = (P("dp", "context", None), P(None, "dp"), P(None, "dp"))
    return jax.shard_map(
        four_by_eight if tuned else any_mesh, mesh=mesh, in_specs=in_specs, out_specs=out_specs, check_vma=False
    )
```
